32 devices in a mesh: seq: 8 (over z, y), head: 4 (over x, core).
Axes of the slice: x: 2, y: 2, z: 4, core: 2. Of those that a mesh axis runs over, the one named last changes fastest.
Arguments:
- queries: bfloat16 [4096, 2048], P('seq', 'head'), may hold values from -6 to 6
- key_vectors: bfloat16 [4096, 2048], P('seq', 'head'), may hold values from -8 to 8
- value_vectors: bfloat16 [4096, 2048], P('seq', 'head'), may hold values from -40 to 40
- norm_gain: float32 [2048], P('head'), may hold values from 0.25 to 1.75
- out_weight: bfloat16 [2048, 2048], P('head'), may hold values from -0.125 to 0.125
Outputs:
- projected: bfloat16 [4096, 2048], P(('seq', 'head'))
The draws below stay inside these ranges and needn't reach their ends.
All inputs are finite; a program needn't handle non-finite values.
Results may differ from the reference program's by a relative error of at most 0.013.
Values may be sent and summed in bfloat16 or wider, within the bound.
No kernel may reach another device: no remote copies, remote signals or barrier semaphores. Data moves between devices by JAX's collectives and lax.ppermute only.
A program may use at most 128 MiB of HBM per device.

```python
import math
import jax
import jax.numpy as jnp
from jax import lax

D = 2048
HEADS = 16
DH = 128
TOKENS = 4096


def draw_key_vectors(key, part):
    key_noise, key_mixing = jax.random.split(jax.random.fold_in(key, 11))
    noise = jax.random.normal(key_noise, (TOKENS, HEADS, DH), jnp.float32)
    mixing = jax.random.normal(key_mixing, (HEADS, DH, DH), jnp.float32) * DH ** (-0.5)
    mixed_keys = jnp.einsum('thd,hde->the', noise, mixing)
    return jnp.clip(mixed_keys, -8.0, 8.0).reshape(TOKENS, HEADS * DH).astype(jnp.bfloat16)


def draw_value_vectors(key, part):
    key_base, key_column = jax.random.split(jax.random.fold_in(key, 23), 2)
    feature_count = HEADS * DH
    column = jnp.exp(jax.random.uniform(key_column, (feature_count,), jnp.float32, 0.0, math.log(10.0)))
    sample = jax.random.normal(key_base, (TOKENS, feature_count), jnp.float32)
    return jnp.clip(sample * column, -40.0, 40.0).astype(jnp.bfloat16)


def level_of(rng, dims, cuts, least, top_value):
    def one(dim, shards_of):
        draws = jax.random.uniform(jax.random.fold_in(jax.random.fold_in(rng, 6), dim), (shards_of,), jnp.float32, least / len(cuts), top_value / len(cuts))
        return jnp.repeat(jnp.exp(draws), dims[dim] // shards_of).reshape((-1,) + (1,) * (len(dims) - dim - 1))

    gain = one(*cuts[0])
    for cut in cuts[1:]:
        gain = gain * one(*cut)
    return gain


def normal_values(key, shape, scale, limit, cuts=(), kind=jnp.bfloat16):
    loudness = level_of(key, shape, cuts, -0.22, 0.18) if cuts else 1.0
    drawn = jax.random.normal(key, shape, jnp.float32) * scale * loudness
    return jnp.minimum(jnp.maximum(drawn, -limit), limit).astype(kind)


def setup_inputs(seed: int = 0) -> dict:
    seeds = jax.random.split(jax.random.key(seed), 6)
    return {
        "queries": normal_values(seeds[0], (TOKENS, HEADS * DH), 1.0, 6.0, ((0, 8), (1, 4))),
        "key_vectors": draw_key_vectors(jax.random.fold_in(seeds[5], 71), 0),
        "value_vectors": draw_value_vectors(jax.random.fold_in(seeds[5], 71), 0),
        "norm_gain": jnp.clip(1.0 + 0.15 * jax.random.normal(seeds[3], (HEADS * DH,), jnp.float32), 0.25, 1.75),
        "out_weight": normal_values(seeds[4], (HEADS * DH, D), (HEADS * DH) ** -0.5, 0.125, ((0, 4),)),
    }


highest = lax.Precision.HIGHEST

def attend_all(queries, key_vectors, value_vectors):
    token_rows = queries.shape[0]
    head_count = queries.shape[1] // DH
    block_len = math.gcd(token_rows, 256)
    block_count = token_rows // block_len

    def blocked(array):
        return array.astype(jnp.float32).reshape(block_count, block_len, head_count, DH)
    position = jnp.arange(block_len)
    lower_mask = (position[None, :] <= position[:, None]).astype(jnp.float32)
    strict_mask = (position[:, None] < position[None, :]).astype(jnp.float32)

    def block_step(carried, block):
        keys_gram, query_value, pair_state = carried
        query_float, key_float, value_float = block
        scores = jnp.einsum('thd,ihd->hti', query_float, key_float, precision=highest)
        paired = jnp.swapaxes(scores, 1, 2) * strict_mask
        inner_pairs = jnp.einsum('hti,hij->htj', scores, paired, precision=highest)
        query_state = jnp.einsum('thd,hde->hte', query_float, keys_gram, precision=highest)
        cross_terms = jnp.einsum('hte,jhe->htj', query_state, query_float, precision=highest)
        mixing = (inner_pairs + cross_terms) * lower_mask
        result = jnp.einsum('htj,jhd->thd', mixing, value_float, precision=highest)
        result = result + jnp.einsum('thd,hde->the', query_float, pair_state, precision=highest)
        gram_block = jnp.einsum('thd,the->hde', key_float, key_float, precision=highest)
        cross_block = jnp.einsum('thd,the->hde', query_float, value_float, precision=highest)
        paired_values = jnp.einsum('hij,jhe->hie', paired, value_float, precision=highest)
        pair_block = jnp.einsum('ihd,hie->hde', key_float, paired_values, precision=highest)
        pair_next = pair_state + pair_block + jnp.einsum('hde,hef->hdf', keys_gram, cross_block, precision=highest)
        return ((keys_gram + gram_block, query_value + cross_block, pair_next), result)
    zero_state = jnp.zeros((head_count, DH, DH), jnp.float32)
    unused, results = lax.scan(block_step, (zero_state, zero_state, zero_state), (blocked(queries), blocked(key_vectors), blocked(value_vectors)))
    return results.reshape(token_rows, head_count, DH)

def reference(queries, key_vectors, value_vectors, norm_gain, out_weight):
    attended = attend_all(queries, key_vectors, value_vectors)
    head_count = attended.shape[1]
    mean_square = lax.optimization_barrier(jnp.mean(attended * attended, axis=-1, keepdims=True))
    normed = attended * lax.rsqrt(mean_square + 1e-06) * norm_gain.reshape(head_count, DH)
    normed = normed.astype(jnp.bfloat16).reshape(attended.shape[0], head_count * DH)
    return jnp.dot(normed, out_weight, preferred_element_type=jnp.float32).astype(jnp.bfloat16)
```

```python
import functools

import jax
import jax.numpy as jnp
from jax import lax
from jax.experimental import pallas as pl
from jax.experimental.pallas import tpu as pltpu
from jax.sharding import PartitionSpec as P

DH = 128
F32 = jnp.float32
BF16 = jnp.bfloat16


def mm(a, b):
    return lax.dot_general(a, b, (((1,), (0,)), ((), ())), preferred_element_type=F32)


def mm_nt(a, b):
    return lax.dot_general(a, b, (((1,), (1,)), ((), ())), preferred_element_type=F32)


def mm_tn(a, b):
    return lax.dot_general(a, b, (((0,), (0,)), ((), ())), preferred_element_type=F32)


def strict_upper(n):
    return lax.broadcasted_iota(jnp.int32, (n, n), 0) < lax.broadcasted_iota(jnp.int32, (n, n), 1)


def lower(n):
    return lax.broadcasted_iota(jnp.int32, (n, n), 0) >= lax.broadcasted_iota(jnp.int32, (n, n), 1)


def cost(flops, data):
    return pl.CostEstimate(flops=int(flops), bytes_accessed=int(data), transcendentals=0)


def smem():
    return pl.BlockSpec(memory_space=pltpu.SMEM)


def head_columns(rows):
    return pl.BlockSpec((rows, DH), lambda h: (0, h))


def per_head(*lead):
    zeros = (0,) * len(lead)
    return pl.BlockSpec((*lead, 1, DH, DH), lambda h: (*zeros, h, 0, 0))


def sums_kernel(q_ref, k_ref, v_ref, own_ref, send_ref):
    k = k_ref[...]
    gram = mm_tn(k, k)
    cross = mm_tn(q_ref[...], v_ref[...])
    own_ref[0, 0] = gram
    own_ref[1, 0] = cross
    send_ref[0, 0] = gram.astype(BF16)
    send_ref[1, 0] = cross.astype(BF16)


def local_sums(q, k, v):
    rows, width = q.shape
    heads = width // DH
    shape = (2, heads, DH, DH)
    return pl.pallas_call(
        sums_kernel,
        grid=(heads,),
        in_specs=[head_columns(rows)] * 3,
        out_specs=[per_head(2)] * 2,
        out_shape=[jax.ShapeDtypeStruct(shape, F32), jax.ShapeDtypeStruct(shape, BF16)],
        cost_estimate=cost(4 * rows * width * DH, 3 * rows * width * 2),
        name="local_sums",
    )(q, k, v)


def pairs_kernel(block, q_ref, k_ref, v_ref, own_ref, send_ref):
    rows = q_ref.shape[0]
    strict = strict_upper(block)
    gram = jnp.zeros((DH, DH), F32)
    pair = jnp.zeros((DH, DH), F32)
    for start in range(0, rows, block):
        q = q_ref[pl.ds(start, block), :]
        k = k_ref[pl.ds(start, block), :]
        v = v_ref[pl.ds(start, block), :]
        paired = jnp.where(strict, mm_nt(k, q), 0.0).astype(BF16)
        pair = pair + mm_tn(k, mm(paired, v).astype(BF16))
        if start:
            pair = pair + mm(gram.astype(BF16), mm_tn(q, v).astype(BF16))
        if start + block < rows:
            gram = gram + mm_tn(k, k)
    own_ref[0] = pair
    send_ref[0] = pair.astype(BF16)


def local_pairs(q, k, v, block):
    rows, width = q.shape
    heads = width // DH
    shape = (heads, DH, DH)
    return pl.pallas_call(
        functools.partial(pairs_kernel, block),
        grid=(heads,),
        in_specs=[head_columns(rows)] * 3,
        out_specs=[per_head()] * 2,
        out_shape=[jax.ShapeDtypeStruct(shape, F32), jax.ShapeDtypeStruct(shape, BF16)],
        cost_estimate=cost(4 * rows * width * block, 3 * rows * width * 2),
        name="local_pairs",
    )(q, k, v)


def union_sums_kernel(upper_ref, own_ref, before_ref, got_ref, own_out, before_out, send_ref):
    upper = upper_ref[0].astype(F32)
    got = got_ref[...].astype(F32)
    total = own_ref[...] + got
    own_out[...] = total
    before_out[...] = before_ref[...] + upper * got
    send_ref[...] = total.astype(BF16)


def union_sums(upper, own, before, got):
    return pl.pallas_call(
        union_sums_kernel,
        in_specs=[smem()] + [pl.BlockSpec(memory_space=pltpu.VMEM)] * 3,
        out_shape=[
            jax.ShapeDtypeStruct(own.shape, F32),
            jax.ShapeDtypeStruct(own.shape, F32),
            jax.ShapeDtypeStruct(own.shape, BF16),
        ],
        cost_estimate=cost(own.size * 4, own.size * 20),
        name="union_sums",
    )(upper, own, before, got)


def union_pairs_kernel(
    upper_ref, own_ref, before_ref, got_ref, sums_ref, ahead_ref, sums_got_ref, own_out, before_out, send_ref
):
    upper = upper_ref[0]
    first = upper == 0
    weight = upper.astype(F32)
    for h in range(own_ref.shape[0]):
        got = got_ref[h].astype(F32)
        left = jnp.where(first, sums_ref[0, h].astype(BF16), sums_got_ref[0, h])
        right = jnp.where(first, sums_got_ref[1, h], sums_ref[1, h].astype(BF16))
        total = own_ref[h] + got + mm(left, right)
        own_out[h] = total
        send_ref[h] = total.astype(BF16)
        ahead = got + mm(sums_got_ref[0, h], ahead_ref[1, h].astype(BF16))
        before_out[h] = before_ref[h] + weight * ahead


def union_pairs(upper, own, before, got, sums, ahead, sums_got):
    return pl.pallas_call(
        union_pairs_kernel,
        in_specs=[smem()] + [pl.BlockSpec(memory_space=pltpu.VMEM)] * 6,
        out_shape=[
            jax.ShapeDtypeStruct(own.shape, F32),
            jax.ShapeDtypeStruct(own.shape, F32),
            jax.ShapeDtypeStruct(own.shape, BF16),
        ],
        cost_estimate=cost(own.size * 4 * DH, own.size * 40),
        name="union_pairs",
    )(upper, own, before, got, sums, ahead, sums_got)


def inner_kernel(block, upper_ref, q_ref, k_ref, v_ref, ahead_ref, got_ref, out_ref):
    rows = q_ref.shape[0]
    strict = strict_upper(block)
    causal = lower(block)
    gram = ahead_ref[0, 0] + upper_ref[0].astype(F32) * got_ref[0].astype(F32)
    pair = jnp.zeros((DH, DH), F32)
    for start in range(0, rows, block):
        q = q_ref[pl.ds(start, block), :]
        k = k_ref[pl.ds(start, block), :]
        v = v_ref[pl.ds(start, block), :]
        scores = mm_nt(q, k).astype(BF16)
        paired = jnp.where(strict, mm_nt(k, q), 0.0).astype(BF16)
        gram_low = gram.astype(BF16)
        state = mm(q, gram_low).astype(BF16)
        mixing = mm(scores, paired) + mm_nt(state, q)
        mixing = jnp.where(causal, mixing, 0.0).astype(BF16)
        result = mm(mixing, v)
        if start:
            result = result + mm(q, pair.astype(BF16))
        out_ref[pl.ds(start, block), :] = result
        if start + block < rows:
            pair = pair + mm_tn(k, mm(paired, v).astype(BF16)) + mm(gram_low, mm_tn(q, v).astype(BF16))
            gram = gram + mm_tn(k, k)


def inner(upper, q, k, v, ahead, got, block):
    rows, width = q.shape
    heads = width // DH
    return pl.pallas_call(
        functools.partial(inner_kernel, block),
        grid=(heads,),
        in_specs=[smem()] + [head_columns(rows)] * 3 + [per_head(2), per_head()],
        out_specs=head_columns(rows),
        out_shape=jax.ShapeDtypeStruct((rows, width), F32),
        cost_estimate=cost(rows * width * (10 * block + 4 * DH), rows * width * 10),
        name="inner",
    )(upper, q, k, v, ahead, got)


def base_kernel(upper_ref, before_ref, ahead_ref, got_ref, out_ref):
    weight = upper_ref[0].astype(F32)
    for h in range(before_ref.shape[0]):
        out_ref[h] = before_ref[h] + weight * mm(got_ref[h], ahead_ref[1, h].astype(BF16))


def base_pairs(upper, before, ahead, got):
    return pl.pallas_call(
        base_kernel,
        in_specs=[smem()] + [pl.BlockSpec(memory_space=pltpu.VMEM)] * 3,
        out_shape=jax.ShapeDtypeStruct(before.shape, F32),
        cost_estimate=cost(before.size * 2 * DH, before.size * 16),
        name="base_pairs",
    )(upper, before, ahead, got)


def normed_kernel(upper_ref, first_ref, q_ref, part_ref, base_ref, got_ref, gain_ref, out_ref):
    weight = upper_ref[0].astype(F32)
    for h in range(base_ref.shape[0]):
        pair = base_ref[h] + weight * got_ref[h].astype(F32)
        at = slice(h * DH, (h + 1) * DH)
        attended = part_ref[:, at] + mm(q_ref[:, at], pair.astype(BF16))
        mean = jnp.mean(attended * attended, axis=-1, keepdims=True)
        normed = attended * lax.rsqrt(mean + 1e-6) * gain_ref[:, at]
        out_ref[0, :, at] = normed.astype(BF16)


def normed_blocks(upper, first, q, part, base, got, gain, blocks):
    rows, width = q.shape
    size = rows // blocks
    heads = width // DH
    row_block = pl.BlockSpec((size, width), lambda j, up, first: (first[0] ^ (2 * j), 0))
    whole = pl.BlockSpec((heads, DH, DH), lambda j, up, first: (0, 0, 0))
    return pl.pallas_call(
        normed_kernel,
        grid_spec=pltpu.PrefetchScalarGridSpec(
            num_scalar_prefetch=2,
            grid=(blocks // 2,),
            in_specs=[row_block, row_block, whole, whole, pl.BlockSpec((1, width), lambda j, up, first: (0, 0))],
            out_specs=pl.BlockSpec((1, size, width), lambda j, up, first: (j, 0, 0)),
        ),
        out_shape=jax.ShapeDtypeStruct((blocks // 2, size, width), BF16),
        cost_estimate=cost(rows * width * DH, rows * width * 4),
        name="normed_blocks",
    )(upper, first, q, part, base, got, gain)


def project_kernel(a_ref, b_ref, wa_ref, wb_ref, out_ref):
    total = mm(a_ref[0], wa_ref[...]) + mm(b_ref[0], wb_ref[...])
    out_ref[...] = total.astype(out_ref.dtype)


def project(index, kept, came, weight, weight_came, dtype):
    blocks, size, width = kept.shape
    columns = weight.shape[1]
    tile = 512 if columns % 512 == 0 else columns
    rows = pl.BlockSpec((1, size, width), lambda c: (index, 0, 0))
    weights = pl.BlockSpec((width, tile), lambda c: (0, c))
    return pl.pallas_call(
        project_kernel,
        grid=(columns // tile,),
        in_specs=[rows, rows, weights, weights],
        out_specs=pl.BlockSpec((size, tile), lambda c: (0, c)),
        out_shape=jax.ShapeDtypeStruct((size, columns), dtype),
        cost_estimate=cost(4 * size * width * columns, 4 * width * columns),
        name="project",
    )(kept, came, weight, weight_came)


def flip(value, axis, bit):
    count = lax.axis_size(axis)
    return lax.ppermute(value, axis, [(i, i ^ bit) for i in range(count)])


def shards(queries, key_vectors, value_vectors, norm_gain, out_weight):
    rows, width = queries.shape
    seq_count, head_count = lax.axis_size("seq"), lax.axis_size("head")
    seq, head = lax.axis_index("seq"), lax.axis_index("head")
    block = 256 if rows % 256 == 0 else rows

    weight_came = flip(out_weight, "head", 1)

    sums, sums_send = local_sums(queries, key_vectors, value_vectors)
    pairs, pairs_send = local_pairs(queries, key_vectors, value_vectors, block)
    ahead = jnp.zeros_like(sums)
    before = jnp.zeros_like(pairs)
    bit = 1
    while 2 * bit < seq_count:
        upper = ((seq // bit) % 2).astype(jnp.int32).reshape(1)
        sums_got = flip(sums_send, "seq", bit)
        pairs_got = flip(pairs_send, "seq", bit)
        pairs, before, pairs_send = union_pairs(upper, pairs, before, pairs_got, sums, ahead, sums_got)
        sums, ahead, sums_send = union_sums(upper, sums, ahead, sums_got)
        bit *= 2
    upper = ((seq // bit) % 2).astype(jnp.int32).reshape(1)
    gram_got = flip(sums_send[0], "seq", bit)
    pairs_got = flip(pairs_send, "seq", bit)
    part = inner(upper, queries, key_vectors, value_vectors, ahead, gram_got, block)
    base = base_pairs(upper, before, ahead, gram_got)

    gain = norm_gain.reshape(1, width)
    mine = head.astype(jnp.int32).reshape(1)
    sent = normed_blocks(upper, mine ^ 1, queries, part, base, pairs_got, gain, head_count)
    came = flip(sent, "head", 1)
    kept = normed_blocks(upper, mine, queries, part, base, pairs_got, gain, head_count)

    count = head_count // 2
    if count == 1:
        return project(0, kept, came, out_weight, weight_came, BF16)
    parts = {}
    for j in reversed(range(count)):
        parts[j] = project(j, kept, came, out_weight, weight_came, BF16 if 2 * j >= count else F32)
    while count > 1:
        count //= 2
        for j in range(count):
            got = flip(parts[count + j].astype(BF16), "head", 2 * count)
            parts[j] = parts[j].astype(F32) + got.astype(F32)
    return parts[0].astype(BF16)


def solution(mesh):
    in_specs = (P("seq", "head"), P("seq", "head"), P("seq", "head"), P("head"), P("head", None))
    out_specs = P(("seq", "head"), None)
    return jax.shard_map(shards, mesh=mesh, in_specs=in_specs, out_specs=out_specs, check_vma=False)
```

```python
import functools

import jax
import jax.numpy as jnp
from jax import lax
from jax.experimental import pallas as pl
from jax.experimental.pallas import tpu as pltpu
from jax.sharding import PartitionSpec as P

DH = 128
DIAG = 16
F32 = jnp.float32
BF16 = jnp.bfloat16


def mm(a, b):
    return lax.dot_general(a, b, (((1,), (0,)), ((), ())), preferred_element_type=F32)


def mm_nt(a, b):
    return lax.dot_general(a, b, (((1,), (1,)), ((), ())), preferred_element_type=F32)


def mm_tn(a, b):
    return lax.dot_general(a, b, (((0,), (0,)), ((), ())), preferred_element_type=F32)


def row_col(n):
    return lax.broadcasted_iota(jnp.int32, (n, n), 0), lax.broadcasted_iota(jnp.int32, (n, n), 1)


def is_upper(bit):
    return lax.bitwise_and(lax.axis_index("seq"), bit) != 0


def columns(h):
    return slice(h * DH, (h + 1) * DH)


def call(kernel, ins, outs, name, flops=0, scratch=(), mib=4):
    arrays = [pltpu.with_memory_space_constraint(a, space) if space is pltpu.HBM else a for a, space in ins]
    data = sum(a.size * a.dtype.itemsize for a in arrays)
    return pl.pallas_call(
        kernel,
        in_specs=[pl.BlockSpec(memory_space=space) for a, space in ins],
        out_specs=[pl.BlockSpec(memory_space=pltpu.VMEM) for o in outs],
        out_shape=[pltpu.VMEM(shape, dtype) for shape, dtype in outs],
        scratch_shapes=list(scratch),
        compiler_params=pltpu.CompilerParams(vmem_limit_bytes=mib << 20),
        cost_estimate=pl.CostEstimate(flops=int(flops), bytes_accessed=int(data), transcendentals=0),
        name=name,
    )(*arrays)


def vm(*arrays):
    return [(a, pltpu.VMEM) for a in arrays]


def pack(send_ref, grams):
    heads = len(grams)
    pairs = (heads + 1) // 2
    row, col = row_col(DH)
    diagonals = []
    for p in range(pairs):
        a, b = grams[2 * p], grams[min(2 * p + 1, heads - 1)]
        send_ref[pl.ds(p * DH, DH), :] = jnp.where(row <= col, a, b).astype(BF16)
        diagonals.append(jnp.sum(jnp.where(row == col, b, 0.0), axis=0, keepdims=True))
    diagonals += [jnp.zeros((1, DH), F32)] * (DIAG - pairs)
    send_ref[pl.ds(pairs * DH, DIAG), :] = jnp.concatenate(diagonals, axis=0).astype(BF16)


def unpack(got_ref, heads):
    pairs = (heads + 1) // 2
    row, col = row_col(DH)
    diagonals = got_ref[pl.ds(pairs * DH, DIAG), :].astype(F32)
    grams = []
    for p in range(pairs):
        m = got_ref[pl.ds(p * DH, DH), :].astype(F32)
        t = m.T
        d = jnp.broadcast_to(diagonals[p : p + 1, :], (DH, DH))
        grams.append(jnp.where(row <= col, m, t))
        grams.append(jnp.where(row > col, m, jnp.where(row < col, t, d)))
    return grams[:heads]


def packed_rows(heads):
    return (heads + 1) // 2 * DH + DIAG


def sums_kernel(chunks, q_hbm, k_hbm, v_hbm, q_ref, k_ref, v_ref, own_ref, send_ref, sem):
    rows, width = q_ref.shape
    heads = width // DH
    size = rows // chunks
    copies = []
    for c in range(chunks):
        at = pl.ds(c * size, size)
        for n, (src, dst) in enumerate(((k_hbm, k_ref), (q_hbm, q_ref), (v_hbm, v_ref))):
            copies.append(pltpu.make_async_copy(src.at[at], dst.at[at], sem.at[c, n]))
    for copy in copies:
        copy.start()
    grams = [None] * heads
    crosses = [None] * heads
    for c in range(chunks):
        at = pl.ds(c * size, size)
        copies[3 * c].wait()
        for h in range(heads):
            k = k_ref[at, columns(h)]
            gram = mm_tn(k, k)
            grams[h] = gram if c == 0 else grams[h] + gram
        copies[3 * c + 1].wait()
        copies[3 * c + 2].wait()
        for h in range(heads):
            cross = mm_tn(q_ref[at, columns(h)], v_ref[at, columns(h)])
            crosses[h] = cross if c == 0 else crosses[h] + cross
    base = packed_rows(heads)
    pack(send_ref, grams)
    for h in range(heads):
        own_ref[0, h] = grams[h]
        own_ref[1, h] = crosses[h]
        send_ref[pl.ds(base + h * DH, DH), :] = crosses[h].astype(BF16)


def local_sums(q, k, v):
    rows, width = q.shape
    heads = width // DH
    chunks = 2 if rows % 32 == 0 else 1
    return call(
        functools.partial(sums_kernel, chunks),
        [(a, pltpu.HBM) for a in (q, k, v)],
        [((rows, width), BF16)] * 3
        + [((2, heads, DH, DH), F32), ((packed_rows(heads) + heads * DH, DH), BF16)],
        "local_sums",
        flops=4 * rows * width * DH,
        scratch=[pltpu.SemaphoreType.DMA((chunks, 3))],
    )


def pairs_kernel(block, q_ref, k_ref, v_ref, own_ref, send_ref):
    rows, width = q_ref.shape
    row, col = row_col(block)
    for h in range(width // DH):
        gram = pair = None
        for start in range(0, rows, block):
            at = pl.ds(start, block)
            q, k, v = q_ref[at, columns(h)], k_ref[at, columns(h)], v_ref[at, columns(h)]
            paired = jnp.where(row < col, mm_nt(k, q), 0.0).astype(BF16)
            here = mm_tn(k, mm(paired, v).astype(BF16))
            if start:
                here = pair + here + mm(gram.astype(BF16), mm_tn(q, v).astype(BF16))
            pair = here
            if start + block < rows:
                more = mm_tn(k, k)
                gram = gram + more if start else more
        own_ref[h] = pair
        send_ref[pl.ds(h * DH, DH), :] = pair.astype(BF16)


def local_pairs(q, k, v, block):
    rows, width = q.shape
    heads = width // DH
    return call(
        functools.partial(pairs_kernel, block),
        vm(q, k, v),
        [((heads, DH, DH), F32), ((heads * DH, DH), BF16)],
        "local_pairs",
        flops=4 * rows * width * block,
    )


def union_sums_kernel(bit, first, last, got_ref, own_ref, *refs):
    refs = list(refs)
    ahead_ref = None if first else refs.pop(0)
    own_out, ahead_out, send_ref, left_ref, right_ref, came_ref = refs
    heads = own_ref.shape[1]
    upper = is_upper(bit)
    weight = upper.astype(F32)
    base = packed_rows(heads)
    totals = []
    for h, gram in enumerate(unpack(got_ref, heads)):
        mine = own_ref[0, h]
        total = mine + gram
        totals.append(total)
        own_out[0, h] = total
        ahead_out[0, h] = weight * gram if first else ahead_ref[0, h] + weight * gram
        left_ref[h] = jnp.where(upper, gram, mine).astype(BF16)
        came_ref[h] = gram.astype(BF16)
    pack(send_ref, totals)
    for h in range(heads):
        cross = got_ref[pl.ds(base + h * DH, DH), :].astype(F32)
        mine = own_ref[1, h]
        total = mine + cross
        own_out[1, h] = total
        ahead_out[1, h] = weight * cross if first else ahead_ref[1, h] + weight * cross
        right_ref[h] = jnp.where(upper, mine, cross).astype(BF16)
        if not last:
            send_ref[pl.ds(base + h * DH, DH), :] = total.astype(BF16)


def union_sums(bit, got, own, ahead, last):
    heads = own.shape[1]
    first = ahead is None
    rows = packed_rows(heads) + (0 if last else heads * DH)
    low = ((heads, DH, DH), BF16)
    return call(
        functools.partial(union_sums_kernel, bit, first, last),
        vm(got, own) + ([] if first else vm(ahead)),
        [(own.shape, F32), (own.shape, F32), ((rows, DH), BF16), low, low, low],
        "union_sums",
    )


def union_pairs_kernel(bit, first, got_ref, own_ref, left_ref, right_ref, *refs):
    refs = list(refs)
    if not first:
        before_ref, came_ref, ahead_ref = refs[:3]
        refs = refs[3:]
    own_out, before_out, send_ref = refs
    weight = is_upper(bit).astype(F32)
    for h in range(own_ref.shape[0]):
        got = got_ref[pl.ds(h * DH, DH), :].astype(F32)
        total = own_ref[h] + got + mm(left_ref[h], right_ref[h])
        own_out[h] = total
        send_ref[pl.ds(h * DH, DH), :] = total.astype(BF16)
        if first:
            before_out[h] = weight * got
        else:
            before_out[h] = before_ref[h] + weight * (got + mm(came_ref[h], ahead_ref[1, h].astype(BF16)))


def union_pairs(bit, got, own, left, right, before, came, ahead):
    first = before is None
    return call(
        functools.partial(union_pairs_kernel, bit, first),
        vm(got, own, left, right) + ([] if first else vm(before, came, ahead)),
        [(own.shape, F32), (own.shape, F32), (got.shape, BF16)],
        "union_pairs",
        flops=own.size * 4 * DH,
    )


def ahead_kernel(bit, got_ref, ahead_ref, before_ref, gram_ref, base_ref):
    weight = is_upper(bit).astype(F32)
    heads = before_ref.shape[0]
    for h, gram in enumerate(unpack(got_ref, heads)):
        gram_ref[h] = (ahead_ref[0, h] + weight * gram).astype(BF16)
        base_ref[h] = before_ref[h] + weight * mm(gram.astype(BF16), ahead_ref[1, h].astype(BF16))


def ahead_of_device(bit, got, ahead, before):
    return call(
        functools.partial(ahead_kernel, bit),
        vm(got, ahead, before),
        [(before.shape, BF16), (before.shape, F32)],
        "ahead_of_device",
        flops=before.size * 2 * DH,
    )


def inner_kernel(block, q_ref, k_ref, v_ref, out_ref):
    rows, width = q_ref.shape
    row, col = row_col(block)
    for h in range(width // DH):
        gram = pair = None
        for start in range(0, rows, block):
            at = pl.ds(start, block)
            q, k, v = q_ref[at, columns(h)], k_ref[at, columns(h)], v_ref[at, columns(h)]
            paired = jnp.where(row < col, mm_nt(k, q), 0.0).astype(BF16)
            mixing = mm(mm_nt(q, k).astype(BF16), paired)
            if start:
                mixing = mixing + mm_nt(mm(q, gram.astype(BF16)).astype(BF16), q)
            result = mm(jnp.where(row >= col, mixing, 0.0).astype(BF16), v)
            if start:
                result = result + mm(q, pair.astype(BF16))
            out_ref[at, columns(h)] = result
            if start + block < rows:
                here = mm_tn(k, mm(paired, v).astype(BF16))
                if start:
                    here = pair + here + mm(gram.astype(BF16), mm_tn(q, v).astype(BF16))
                pair = here
                more = mm_tn(k, k)
                gram = gram + more if start else more


def inner(q, k, v, block):
    rows, width = q.shape
    return call(
        functools.partial(inner_kernel, block),
        vm(q, k, v),
        [((rows, width), F32)],
        "inner",
        flops=rows * width * 8 * block,
    )[0]


def outer_kernel(block, q_ref, v_ref, gram_ref, part_ref, out_ref):
    rows, width = q_ref.shape
    row, col = row_col(block)
    for h in range(width // DH):
        cross = None
        for start in range(0, rows, block):
            at = pl.ds(start, block)
            q, v = q_ref[at, columns(h)], v_ref[at, columns(h)]
            state = mm(q, gram_ref[h]).astype(BF16)
            mixing = jnp.where(row >= col, mm_nt(state, q), 0.0).astype(BF16)
            result = part_ref[at, columns(h)] + mm(mixing, v)
            if start:
                result = result + mm(state, cross.astype(BF16))
            out_ref[at, columns(h)] = result
            if start + block < rows:
                more = mm_tn(q, v)
                cross = cross + more if start else more


def outer(q, v, gram, part, block):
    rows, width = q.shape
    return call(
        functools.partial(outer_kernel, block),
        vm(q, v, gram, part),
        [((rows, width), F32)],
        "outer",
        flops=rows * width * 6 * block,
    )[0]


def normed_kernel(bit, blocks, other, q_ref, part_ref, base_ref, got_ref, gain_ref, out_ref):
    weight = is_upper(bit).astype(F32)
    size = q_ref.shape[0] // blocks
    first = lax.bitwise_xor(lax.axis_index("head"), other)
    for h in range(base_ref.shape[0]):
        pair = (base_ref[h] + weight * got_ref[pl.ds(h * DH, DH), :].astype(F32)).astype(BF16)
        for j in range(blocks // 2):
            at = pl.ds(pl.multiple_of(lax.bitwise_xor(first, 2 * j) * size, size), size)
            attended = part_ref[at, columns(h)] + mm(q_ref[at, columns(h)], pair)
            mean = jnp.mean(attended * attended, axis=-1, keepdims=True)
            normed = attended * lax.rsqrt(mean + 1e-6) * gain_ref[:, columns(h)]
            out_ref[j, :, columns(h)] = normed.astype(BF16)


def normed_blocks(bit, other, q, part, base, got, gain, blocks):
    rows, width = q.shape
    return call(
        functools.partial(normed_kernel, bit, blocks, other),
        vm(q, part, base, got, gain),
        [((blocks // 2, rows // blocks, width), BF16)],
        "normed_blocks",
        flops=rows * width * DH,
    )[0]


def project_kernel(index, a_ref, b_ref, wa_ref, wb_ref, out_ref):
    size = out_ref.shape[1]
    tile = 512 if size % 512 == 0 else size
    for start in range(0, size, tile):
        at = slice(start, start + tile)
        total = mm(a_ref[index], wa_ref[:, at]) + mm(b_ref[index], wb_ref[:, at])
        out_ref[:, at] = total.astype(out_ref.dtype)


def project(index, kept, came, weight, weight_came, dtype):
    blocks, size, width = kept.shape
    return call(
        functools.partial(project_kernel, index),
        vm(kept, came, weight, weight_came),
        [((size, weight.shape[1]), dtype)],
        "project",
        flops=4 * size * width * weight.shape[1],
        mib=12,
    )[0]


def flip(value, axis, bit):
    count = lax.axis_size(axis)
    return lax.ppermute(value, axis, [(i, i ^ bit) for i in range(count)])


def shards(queries, key_vectors, value_vectors, norm_gain, out_weight):
    rows, width = queries.shape
    seq_count, head_count = lax.axis_size("seq"), lax.axis_size("head")
    block = 256 if rows % 256 == 0 else rows

    q, k, v, sums, sums_send = local_sums(queries, key_vectors, value_vectors)
    pairs, pairs_send = local_pairs(q, k, v, block)
    part = inner(q, k, v, block)
    weight_came = flip(out_weight, "head", 1)
    ahead = before = None
    bit = 1
    while 2 * bit < seq_count:
        sums_got = flip(sums_send, "seq", bit)
        pairs_got = flip(pairs_send, "seq", bit)
        old = ahead
        sums, ahead, sums_send, left, right, came = union_sums(
            bit, sums_got, sums, ahead, 4 * bit >= seq_count
        )
        pairs, before, pairs_send = union_pairs(bit, pairs_got, pairs, left, right, before, came, old)
        bit *= 2
    gram_got = flip(sums_send, "seq", bit)
    pairs_got = flip(pairs_send, "seq", bit)
    gram, base = ahead_of_device(bit, gram_got, ahead, before)
    part = outer(q, v, gram, part, block)

    gain = norm_gain.reshape(1, width)
    sent = normed_blocks(bit, 1, q, part, base, pairs_got, gain, head_count)
    came = flip(sent, "head", 1)
    kept = normed_blocks(bit, 0, q, part, base, pairs_got, gain, head_count)

    count = head_count // 2
    if count == 1:
        return project(0, kept, came, out_weight, weight_came, BF16)
    parts = {}
    for j in reversed(range(count)):
        parts[j] = project(j, kept, came, out_weight, weight_came, BF16 if 2 * j >= count else F32)
    while count > 1:
        count //= 2
        for j in range(count):
            got = flip(parts[count + j].astype(BF16), "head", 2 * count)
            parts[j] = parts[j].astype(F32) + got.astype(F32)
    return parts[0].astype(BF16)


def solution(mesh):
    in_specs = (P("seq", "head"), P("seq", "head"), P("seq", "head"), P("head"), P("head", None))
    out_specs = P(("seq", "head"), None)
    return jax.shard_map(shards, mesh=mesh, in_specs=in_specs, out_specs=out_specs, check_vma=False)
```

```python
import functools

import jax
import jax.numpy as jnp
from jax import lax
from jax.experimental import pallas as pl
from jax.experimental.pallas import tpu as pltpu
from jax.sharding import PartitionSpec as P


DH = 128
DIAG = 16
F32 = jnp.float32
BF16 = jnp.bfloat16


def mm(a, b):
    return lax.dot_general(a, b, (((1,), (0,)), ((), ())), preferred_element_type=F32)


def mm_nt(a, b):
    return lax.dot_general(a, b, (((1,), (1,)), ((), ())), preferred_element_type=F32)


def mm_tn(a, b):
    return lax.dot_general(a, b, (((0,), (0,)), ((), ())), preferred_element_type=F32)


def row_col(n):
    return lax.broadcasted_iota(jnp.int32, (n, n), 0), lax.broadcasted_iota(jnp.int32, (n, n), 1)


def is_upper(bit):
    return lax.bitwise_and(lax.axis_index("seq"), bit) != 0


def columns(h):
    return slice(h * DH, (h + 1) * DH)


def call(kernel, ins, outs, flops=0, scratch=(), mib=4):
    arrays = [pltpu.with_memory_space_constraint(a, space) if space is pltpu.HBM else a for a, space in ins]
    data = sum(a.size * a.dtype.itemsize for a in arrays)
    return pl.pallas_call(
        kernel,
        in_specs=[pl.BlockSpec(memory_space=space) for a, space in ins],
        out_specs=[pl.BlockSpec(memory_space=pltpu.VMEM) for o in outs],
        out_shape=[pltpu.VMEM(shape, dtype) for shape, dtype in outs],
        scratch_shapes=list(scratch),
        compiler_params=pltpu.CompilerParams(vmem_limit_bytes=mib << 20),
        cost_estimate=pl.CostEstimate(flops=int(flops), bytes_accessed=int(data), transcendentals=0),
    )(*arrays)


def vm(*arrays):
    return [(a, pltpu.VMEM) for a in arrays]


def pack(send_ref, grams):
    heads = len(grams)
    pairs = (heads + 1) // 2
    row, col = row_col(DH)
    diagonals = []
    for p in range(pairs):
        a, b = grams[2 * p], grams[min(2 * p + 1, heads - 1)]
        send_ref[pl.ds(p * DH, DH), :] = jnp.where(row <= col, a, b).astype(BF16)
        diagonals.append(jnp.sum(jnp.where(row == col, b, 0.0), axis=0, keepdims=True))
    diagonals += [jnp.zeros((1, DH), F32)] * (DIAG - pairs)
    send_ref[pl.ds(pairs * DH, DIAG), :] = jnp.concatenate(diagonals, axis=0).astype(BF16)


def unpack(got_ref, heads):
    pairs = (heads + 1) // 2
    row, col = row_col(DH)
    diagonals = got_ref[pl.ds(pairs * DH, DIAG), :].astype(F32)
    grams = []
    for p in range(pairs):
        m = got_ref[pl.ds(p * DH, DH), :].astype(F32)
        t = m.T
        d = jnp.broadcast_to(diagonals[p : p + 1, :], (DH, DH))
        grams.append(jnp.where(row <= col, m, t))
        grams.append(jnp.where(row > col, m, jnp.where(row < col, t, d)))
    return grams[:heads]


def packed_rows(heads):
    return (heads + 1) // 2 * DH + DIAG


def sums_kernel(chunks, q_hbm, k_hbm, v_hbm, w_hbm, q_ref, k_ref, v_ref, own_ref, send_ref, *refs):
    *w_refs, sem, w_sem = refs
    rows, width = q_ref.shape
    heads = width // DH
    size = rows // chunks
    copies = []
    for c in range(chunks):
        at = pl.ds(c * size, size)
        for n, (src, dst) in enumerate(((k_hbm, k_ref), (q_hbm, q_ref), (v_hbm, v_ref))):
            copies.append(pltpu.make_async_copy(src.at[at], dst.at[at], sem.at[c, n]))
    share = w_refs[0].shape[0]
    first = lax.bitwise_and(lax.axis_index("seq"), 1) * len(w_refs)
    for n, w_ref in enumerate(w_refs):
        at = pl.multiple_of((first + n) * share, share)
        copies.append(pltpu.make_async_copy(w_hbm.at[pl.ds(at, share)], w_ref, w_sem.at[n]))
    for copy in copies:
        copy.start()
    grams = [None] * heads
    crosses = [None] * heads
    for c in range(chunks):
        at = pl.ds(c * size, size)
        copies[3 * c].wait()
        for h in range(heads):
            k = k_ref[at, columns(h)]
            gram = mm_tn(k, k)
            grams[h] = gram if c == 0 else grams[h] + gram
        copies[3 * c + 1].wait()
        copies[3 * c + 2].wait()
        for h in range(heads):
            cross = mm_tn(q_ref[at, columns(h)], v_ref[at, columns(h)])
            crosses[h] = cross if c == 0 else crosses[h] + cross
    base = packed_rows(heads)
    pack(send_ref, grams)
    for h in range(heads):
        own_ref[0, h] = grams[h]
        own_ref[1, h] = crosses[h]
        send_ref[pl.ds(base + h * DH, DH), :] = crosses[h].astype(BF16)
    for copy in copies[3 * chunks :]:
        copy.wait()


def local_sums(q, k, v, weight, share, shares):
    rows, width = q.shape
    heads = width // DH
    chunks = 2 if rows % 32 == 0 else 1
    return call(
        functools.partial(sums_kernel, chunks),
        [(a, pltpu.HBM) for a in (q, k, v, weight)],
        [((rows, width), BF16)] * 3
        + [((2, heads, DH, DH), F32), ((packed_rows(heads) + heads * DH, DH), BF16)]
        + [((share, weight.shape[1]), BF16)] * shares,
        flops=4 * rows * width * DH,
        scratch=[pltpu.SemaphoreType.DMA((chunks, 3)), pltpu.SemaphoreType.DMA((shares,))],
        mib=6,
    )


def pairs_kernel(block, q_ref, k_ref, v_ref, w_hbm, own_ref, send_ref, w_ref, w_sem):
    rest = w_ref.shape[0]
    copy = pltpu.make_async_copy(w_hbm.at[pl.ds(w_hbm.shape[0] - rest, rest)], w_ref, w_sem)
    copy.start()
    rows, width = q_ref.shape
    row, col = row_col(block)
    for h in range(width // DH):
        gram = pair = None
        for start in range(0, rows, block):
            at = pl.ds(start, block)
            q, k, v = q_ref[at, columns(h)], k_ref[at, columns(h)], v_ref[at, columns(h)]
            paired = jnp.where(row < col, mm_nt(k, q), 0.0).astype(BF16)
            here = mm_tn(k, mm(paired, v).astype(BF16))
            if start:
                here = pair + here + mm(gram.astype(BF16), mm_tn(q, v).astype(BF16))
            pair = here
            if start + block < rows:
                more = mm_tn(k, k)
                gram = gram + more if start else more
        own_ref[h] = pair
        send_ref[pl.ds(h * DH, DH), :] = pair.astype(BF16)
    copy.wait()


def local_pairs(q, k, v, weight, rest, block):
    rows, width = q.shape
    heads = width // DH
    return call(
        functools.partial(pairs_kernel, block),
        vm(q, k, v) + [(weight, pltpu.HBM)],
        [((heads, DH, DH), F32), ((heads * DH, DH), BF16), ((rest, weight.shape[1]), BF16)],
        flops=4 * rows * width * block,
        scratch=[pltpu.SemaphoreType.DMA],
    )


def union_sums_kernel(bit, first, last, got_ref, own_ref, *refs):
    refs = list(refs)
    ahead_ref = None if first else refs.pop(0)
    ahead_out, send_ref, left_ref, right_ref, came_ref = refs[:5]
    own_out = None if last else refs[5]
    heads = own_ref.shape[1]
    upper = is_upper(bit)
    weight = upper.astype(F32)
    base = packed_rows(heads)
    totals = []
    for h, gram in enumerate(unpack(got_ref, heads)):
        mine = own_ref[0, h]
        total = mine + gram
        totals.append(total)
        if not last:
            own_out[0, h] = total
        ahead_out[0, h] = weight * gram if first else ahead_ref[0, h] + weight * gram
        left_ref[h] = jnp.where(upper, gram, mine).astype(BF16)
        came_ref[h] = gram.astype(BF16)
    pack(send_ref, totals)
    for h in range(heads):
        cross = got_ref[pl.ds(base + h * DH, DH), :].astype(F32)
        mine = own_ref[1, h]
        total = mine + cross
        ahead_out[1, h] = weight * cross if first else ahead_ref[1, h] + weight * cross
        right_ref[h] = jnp.where(upper, mine, cross).astype(BF16)
        if not last:
            own_out[1, h] = total
            send_ref[pl.ds(base + h * DH, DH), :] = total.astype(BF16)


def union_sums(bit, got, own, ahead, last):
    heads = own.shape[1]
    first = ahead is None
    rows = packed_rows(heads) + (0 if last else heads * DH)
    low = ((heads, DH, DH), BF16)
    return call(
        functools.partial(union_sums_kernel, bit, first, last),
        vm(got, own) + ([] if first else vm(ahead)),
        [(own.shape, F32), ((rows, DH), BF16), low, low, low] + ([] if last else [(own.shape, F32)]),
    )


def union_pairs_kernel(bit, first, last, got_ref, own_ref, left_ref, right_ref, *refs):
    refs = list(refs)
    if not first:
        before_ref, came_ref, ahead_ref = refs[:3]
        refs = refs[3:]
    before_out, send_ref = refs[:2]
    weight = is_upper(bit).astype(F32)
    for h in range(own_ref.shape[0]):
        got = got_ref[pl.ds(h * DH, DH), :].astype(F32)
        total = own_ref[h] + got + mm(left_ref[h], right_ref[h])
        if not last:
            refs[2][h] = total
        send_ref[pl.ds(h * DH, DH), :] = total.astype(BF16)
        if first:
            before_out[h] = weight * got
        else:
            before_out[h] = before_ref[h] + weight * (got + mm(came_ref[h], ahead_ref[1, h].astype(BF16)))


def union_pairs(bit, got, own, left, right, before, came, ahead, last):
    first = before is None
    return call(
        functools.partial(union_pairs_kernel, bit, first, last),
        vm(got, own, left, right) + ([] if first else vm(before, came, ahead)),
        [(own.shape, F32), (got.shape, BF16)] + ([] if last else [(own.shape, F32)]),
        flops=own.size * 4 * DH,
    )


def ahead_kernel(bit, got_ref, ahead_ref, before_ref, gram_ref, base_ref):
    weight = is_upper(bit).astype(F32)
    heads = before_ref.shape[0]
    for h, gram in enumerate(unpack(got_ref, heads)):
        gram_ref[h] = (ahead_ref[0, h] + weight * gram).astype(BF16)
        base_ref[h] = before_ref[h] + weight * mm(gram.astype(BF16), ahead_ref[1, h].astype(BF16))


def ahead_of_device(bit, got, ahead, before):
    return call(
        functools.partial(ahead_kernel, bit),
        vm(got, ahead, before),
        [(before.shape, BF16), (before.shape, F32)],
        flops=before.size * 2 * DH,
    )


def inner_kernel(block, heads, q_ref, k_ref, v_ref, out_ref):
    rows = q_ref.shape[0]
    row, col = row_col(block)
    for n, h in enumerate(heads):
        gram = pair = None
        for start in range(0, rows, block):
            at = pl.ds(start, block)
            q, k, v = q_ref[at, columns(h)], k_ref[at, columns(h)], v_ref[at, columns(h)]
            paired = jnp.where(row < col, mm_nt(k, q), 0.0).astype(BF16)
            mixing = mm(mm_nt(q, k).astype(BF16), paired)
            if start:
                mixing = mixing + mm_nt(mm(q, gram.astype(BF16)).astype(BF16), q)
            result = mm(jnp.where(row >= col, mixing, 0.0).astype(BF16), v)
            if start:
                result = result + mm(q, pair.astype(BF16))
            out_ref[at, columns(n)] = result
            if start + block < rows:
                here = mm_tn(k, mm(paired, v).astype(BF16))
                if start:
                    here = pair + here + mm(gram.astype(BF16), mm_tn(q, v).astype(BF16))
                pair = here
                more = mm_tn(k, k)
                gram = gram + more if start else more


def inner(q, k, v, block, heads):
    rows = q.shape[0]
    return call(
        functools.partial(inner_kernel, block, heads),
        vm(q, k, v),
        [((rows, len(heads) * DH), F32)],
        flops=rows * len(heads) * DH * 8 * block,
    )[0]


def outer_kernel(block, q_ref, v_ref, gram_ref, *refs):
    *part_refs, out_ref = refs
    rows = q_ref.shape[0]
    row, col = row_col(block)
    parts = [(ref, n) for ref in part_refs for n in range(ref.shape[1] // DH)]
    for h, (part_ref, n) in enumerate(parts):
        cross = None
        for start in range(0, rows, block):
            at = pl.ds(start, block)
            q, v = q_ref[at, columns(h)], v_ref[at, columns(h)]
            state = mm(q, gram_ref[h]).astype(BF16)
            mixing = jnp.where(row >= col, mm_nt(state, q), 0.0).astype(BF16)
            result = part_ref[at, columns(n)] + mm(mixing, v)
            if start:
                result = result + mm(state, cross.astype(BF16))
            out_ref[at, columns(h)] = result
            if start + block < rows:
                more = mm_tn(q, v)
                cross = cross + more if start else more


def outer(q, v, gram, parts, block):
    rows, width = q.shape
    return call(
        functools.partial(outer_kernel, block),
        vm(q, v, gram, *parts),
        [((rows, width), F32)],
        flops=rows * width * 6 * block,
    )[0]


def normed_kernel(bit, blocks, other, q_ref, part_ref, base_ref, got_ref, gain_ref, out_ref):
    weight = is_upper(bit).astype(F32)
    size = q_ref.shape[0] // blocks
    first = lax.bitwise_xor(lax.axis_index("head"), other)
    for h in range(base_ref.shape[0]):
        pair = (base_ref[h] + weight * got_ref[pl.ds(h * DH, DH), :].astype(F32)).astype(BF16)
        for j in range(blocks // 2):
            at = pl.ds(pl.multiple_of(lax.bitwise_xor(first, j) * size, size), size)
            attended = part_ref[at, columns(h)] + mm(q_ref[at, columns(h)], pair)
            mean = jnp.mean(attended * attended, axis=-1, keepdims=True)
            normed = attended * lax.rsqrt(mean + 1e-6) * gain_ref[:, columns(h)]
            out_ref[j, :, columns(h)] = normed.astype(BF16)


def normed_blocks(bit, other, q, part, base, got, gain, blocks):
    rows, width = q.shape
    return call(
        functools.partial(normed_kernel, bit, blocks, other),
        vm(q, part, base, got, gain),
        [((blocks // 2, rows // blocks, width), BF16)],
        flops=rows * width * DH,
    )[0]


def weights_kernel(shares, *refs):
    *parts, rest_ref, out_ref = refs
    share = parts[0].shape[0]
    odd = lax.bitwise_and(lax.axis_index("seq"), 1)
    for n in range(shares):
        for first, ref in ((odd, parts[n]), (1 - odd, parts[shares + n])):
            at = pl.multiple_of((first * shares + n) * share, share)
            out_ref[pl.ds(at, share), :] = ref[...]
    out_ref[pl.ds(2 * shares * share, rest_ref.shape[0]), :] = rest_ref[...]


def join_weights(direct, neighbour, rest):
    rows = (len(direct) + len(neighbour)) * direct[0].shape[0] + rest.shape[0]
    return call(
        functools.partial(weights_kernel, len(direct)),
        vm(*direct, *neighbour, rest),
        [((rows, rest.shape[1]), BF16)],
        mib=8,
    )[0]


def project_own_kernel(kept_ref, w_ref, out_ref):
    blocks, size, width = kept_ref.shape
    kept = kept_ref[...].reshape(blocks * size, width)
    span = out_ref.shape[2]
    tile = 512 if span % 512 == 0 else span
    for start in range(0, span, tile):
        at = slice(start, start + tile)
        out_ref[:, :, at] = mm(kept, w_ref[:, at]).reshape(blocks, size, tile)


def project_own(kept, weight):
    blocks, size, width = kept.shape
    span = weight.shape[1]
    return call(
        project_own_kernel,
        vm(kept, weight),
        [((blocks, size, span), F32)],
        flops=2 * blocks * size * width * span,
        mib=8,
    )[0]


def project_kernel(index, own_ref, came_ref, w_ref, out_ref):
    span = out_ref.shape[1]
    tile = 512 if span % 512 == 0 else span
    for start in range(0, span, tile):
        at = slice(start, start + tile)
        out_ref[:, at] = (own_ref[index, :, at] + mm(came_ref[index], w_ref[:, at])).astype(out_ref.dtype)


def project(index, own, came, weight, dtype):
    _, size, span = own.shape
    return call(
        functools.partial(project_kernel, index),
        vm(own, came, weight),
        [((size, span), dtype)],
        flops=2 * size * came.shape[2] * span,
        mib=8,
    )[0]


def flip(value, axis, bit):
    count = lax.axis_size(axis)
    return lax.ppermute(value, axis, [(i, i ^ bit) for i in range(count)])


def shards(queries, key_vectors, value_vectors, norm_gain, out_weight):
    rows, width = queries.shape
    seq_count, head_count = lax.axis_size("seq"), lax.axis_size("head")
    block = 256 if rows % 256 == 0 else rows

    top = head_count // 2
    features = out_weight.shape[0]
    shares = 2
    share = features * 3 // 8 // shares // 16 * 16

    q, k, v, sums, sums_send, *weight_shares = local_sums(
        queries, key_vectors, value_vectors, out_weight, share, shares
    )
    pairs, pairs_send, weight_rest = local_pairs(
        q, k, v, out_weight, features - 2 * shares * share, block
    )
    direct = [flip(w, "head", top) for w in weight_shares]
    neighbour = [flip(w, "seq", 1) for w in direct]
    rest = flip(weight_rest, "head", top)
    heads = width // DH
    parts = [
        inner(q, k, v, block, tuple(range(at, min(at + (heads + 1) // 2, heads))))
        for at in range(0, heads, (heads + 1) // 2)
    ]
    ahead = before = None
    bit = 1
    while 2 * bit < seq_count:
        sums_got = flip(sums_send, "seq", bit)
        pairs_got = flip(pairs_send, "seq", bit)
        old = ahead
        last = 4 * bit >= seq_count
        ahead, sums_send, left, right, came, *more = union_sums(bit, sums_got, sums, ahead, last)
        before, pairs_send, *more_pairs = union_pairs(
            bit, pairs_got, pairs, left, right, before, came, old, last
        )
        if not last:
            (pairs,) = more_pairs
            (sums,) = more
        bit *= 2
    gram_got = flip(sums_send, "seq", bit)
    pairs_got = flip(pairs_send, "seq", bit)
    gram, base = ahead_of_device(bit, gram_got, ahead, before)
    part = outer(q, v, gram, parts, block)

    gain = norm_gain.reshape(1, width)
    sent = normed_blocks(bit, top, q, part, base, pairs_got, gain, head_count)
    came = flip(sent, "head", top)
    kept = normed_blocks(bit, 0, q, part, base, pairs_got, gain, head_count)
    own = project_own(kept, out_weight)
    weight_came = join_weights(direct, neighbour, rest)

    count = top
    if count == 1:
        return project(0, own, came, weight_came, BF16)
    results = {
        j: project(j, own, came, weight_came, BF16 if 2 * j >= count else F32) for j in reversed(range(count))
    }
    while count > 1:
        count //= 2
        for j in range(count):
            got = flip(results[count + j].astype(BF16), "head", count)
            results[j] = results[j].astype(F32) + got.astype(F32)
    return results[0].astype(BF16)


def solution(mesh):
    in_specs = (P("seq", "head"), P("seq", "head"), P("seq", "head"), P("head"), P("head", None))
    out_specs = P(("seq", "head"), None)

    return jax.shard_map(shards, mesh=mesh, in_specs=in_specs, out_specs=out_specs, check_vma=False)
```

```python
import functools

import jax
import jax.numpy as jnp
from jax import lax
from jax.experimental import pallas as pl
from jax.experimental.pallas import tpu as pltpu
from jax.sharding import PartitionSpec as P


DH = 128
DIAG = 16
SHARES = (5, 5, 4)
F32 = jnp.float32
BF16 = jnp.bfloat16


def mm(a, b):
    return lax.dot_general(a, b, (((1,), (0,)), ((), ())), preferred_element_type=F32)


def mm_nt(a, b):
    return lax.dot_general(a, b, (((1,), (1,)), ((), ())), preferred_element_type=F32)


def mm_tn(a, b):
    return lax.dot_general(a, b, (((0,), (0,)), ((), ())), preferred_element_type=F32)


def row_col(n):
    return lax.broadcasted_iota(jnp.int32, (n, n), 0), lax.broadcasted_iota(jnp.int32, (n, n), 1)


def is_upper(bit):
    return lax.bitwise_and(lax.axis_index("seq"), bit) != 0


def columns(h):
    return slice(h * DH, (h + 1) * DH)


def call(kernel, ins, outs, flops=0, scratch=(), mib=4):
    arrays = [pltpu.with_memory_space_constraint(a, space) if space is pltpu.HBM else a for a, space in ins]
    data = sum(a.size * a.dtype.itemsize for a in arrays)
    return pl.pallas_call(
        kernel,
        in_specs=[pl.BlockSpec(memory_space=space) for a, space in ins],
        out_specs=[pl.BlockSpec(memory_space=pltpu.VMEM) for o in outs],
        out_shape=[pltpu.VMEM(shape, dtype) for shape, dtype in outs],
        scratch_shapes=list(scratch),
        compiler_params=pltpu.CompilerParams(vmem_limit_bytes=mib << 20),
        cost_estimate=pl.CostEstimate(flops=int(flops), bytes_accessed=int(data), transcendentals=0),
    )(*arrays)


def vm(*arrays):
    return [(a, pltpu.VMEM) for a in arrays]


def pack(grams):
    heads = len(grams)
    row, col = row_col(DH)
    parts, diagonals = [], []
    for p in range(0, heads, 2):
        a, b = grams[p], grams[min(p + 1, heads - 1)]
        parts.append(jnp.where(row <= col, a, b))
        diagonals.append(jnp.sum(jnp.where(row == col, b, 0.0), axis=0, keepdims=True))
    diagonals += [jnp.zeros((1, DH), F32)] * (DIAG - len(diagonals))
    return parts, jnp.concatenate(diagonals, axis=0)


def unpack(rows_of, heads):
    pairs = (heads + 1) // 2
    row, col = row_col(DH)
    diagonals = rows_of(pairs * DH, DIAG)
    grams = []
    for p in range(pairs):
        m = rows_of(p * DH, DH)
        t = m.T
        d = jnp.broadcast_to(diagonals[p : p + 1, :], (DH, DH))
        grams.append(jnp.where(row <= col, m, t))
        grams.append(jnp.where(row > col, m, jnp.where(row < col, t, d)))
    return grams[:heads]


def packed_rows(heads):
    return (heads + 1) // 2 * DH + DIAG


def sums_kernel(chunks, q_hbm, k_hbm, v_hbm, w_hbm, q_ref, k_ref, v_ref, own_ref, send_ref, *refs):
    *w_refs, sem, w_sem = refs
    rows, width = q_ref.shape
    heads = width // DH
    size = rows // chunks
    copies = []
    for c in range(chunks):
        at = pl.ds(c * size, size)
        for n, (src, dst) in enumerate(((k_hbm, k_ref), (q_hbm, q_ref), (v_hbm, v_ref))):
            copies.append(pltpu.make_async_copy(src.at[at], dst.at[at], sem.at[c, n]))
    sizes = [ref.shape[0] for ref in w_refs]
    first = lax.bitwise_and(lax.axis_index("seq"), 1) * sum(sizes)
    for n, w_ref in enumerate(w_refs):
        at = pl.multiple_of(first + sum(sizes[:n]), 16)
        copies.append(pltpu.make_async_copy(w_hbm.at[pl.ds(at, sizes[n])], w_ref, w_sem.at[n]))
    for copy in copies:
        copy.start()
    grams = [None] * heads
    crosses = [None] * heads
    for c in range(chunks):
        at = pl.ds(c * size, size)
        copies[3 * c].wait()
        for h in range(heads):
            k = k_ref[at, columns(h)]
            gram = mm_tn(k, k)
            grams[h] = gram if c == 0 else grams[h] + gram
        copies[3 * c + 1].wait()
        copies[3 * c + 2].wait()
        for h in range(heads):
            cross = mm_tn(q_ref[at, columns(h)], v_ref[at, columns(h)])
            crosses[h] = cross if c == 0 else crosses[h] + cross
    parts, diagonals = pack(grams)
    base = packed_rows(heads)
    places = [(p * DH, part) for p, part in enumerate(parts)] + [(base - DIAG, diagonals)]
    for at, part in places + [(base + h * DH, cross) for h, cross in enumerate(crosses)]:
        own_ref[pl.ds(at, part.shape[0]), :] = part
        send_ref[pl.ds(at, part.shape[0]), :] = part.astype(BF16)
    for copy in copies[3 * chunks :]:
        copy.wait()


def local_sums(q, k, v, weight, sizes):
    rows, width = q.shape
    heads = width // DH
    chunks = 2 if rows % 32 == 0 else 1
    return call(
        functools.partial(sums_kernel, chunks),
        [(a, pltpu.HBM) for a in (q, k, v, weight)],
        [((rows, width), BF16)] * 3
        + [((packed_rows(heads) + heads * DH, DH), dtype) for dtype in (F32, BF16)]
        + [((size, weight.shape[1]), BF16) for size in sizes],
        flops=4 * rows * width * DH,
        scratch=[pltpu.SemaphoreType.DMA((chunks, 3)), pltpu.SemaphoreType.DMA((len(sizes),))],
        mib=6,
    )


def pairs_kernel(block, q_ref, k_ref, v_ref, w_hbm, own_ref, send_ref, paired_ref, w_ref, w_sem):
    rest = w_ref.shape[0]
    copy = pltpu.make_async_copy(w_hbm.at[pl.ds(w_hbm.shape[0] - rest, rest)], w_ref, w_sem)
    copy.start()
    rows, width = q_ref.shape
    for h in range(width // DH):
        pair = None
        for start in range(0, rows, block):
            span = rows - start
            at, on = pl.ds(start, block), pl.ds(start, span)
            k = k_ref[at, columns(h)]
            row = lax.broadcasted_iota(jnp.int32, (block, span), 0)
            col = lax.broadcasted_iota(jnp.int32, (block, span), 1)
            paired = jnp.where(row < col, mm_nt(k, q_ref[on, columns(h)]), 0.0).astype(BF16)
            paired_ref[h, at, start:rows] = paired
            here = mm_tn(k, mm(paired, v_ref[on, columns(h)]).astype(BF16))
            pair = pair + here if start else here
        own_ref[h] = pair
        send_ref[pl.ds(h * DH, DH), :] = pair.astype(BF16)
    copy.wait()


def local_pairs(q, k, v, weight, rest, block):
    rows, width = q.shape
    heads = width // DH
    return call(
        functools.partial(pairs_kernel, block),
        vm(q, k, v) + [(weight, pltpu.HBM)],
        [
            ((heads, DH, DH), F32),
            ((heads * DH, DH), BF16),
            ((heads, rows, rows), BF16),
            ((rest, weight.shape[1]), BF16),
        ],
        flops=4 * rows * width * block,
        scratch=[pltpu.SemaphoreType.DMA],
        mib=8,
    )


def union_sums_kernel(bit, first, last, got_ref, own_ref, *refs):
    refs = list(refs)
    ahead_ref = None if first else refs.pop(0)
    ahead_out, send_ref = refs[:2]
    got = got_ref[...].astype(F32)
    total = own_ref[...] + got
    sent = send_ref.shape[0]
    send_ref[...] = total[:sent].astype(BF16)
    if not last:
        refs[2][...] = total
    ahead = is_upper(bit).astype(F32) * got
    ahead_out[...] = ahead if first else ahead_ref[...] + ahead


def union_sums(bit, got, own, ahead, heads, last):
    first = ahead is None
    sent = packed_rows(heads) if last else got.shape[0]
    return call(
        functools.partial(union_sums_kernel, bit, first, last),
        vm(got, own) + ([] if first else vm(ahead)),
        [(own.shape, F32), ((sent, DH), BF16)] + ([] if last else [(own.shape, F32)]),
    )


def union_pairs_kernel(bit, first, last, got_ref, own_ref, sums_got_ref, sums_ref, *refs):
    refs = list(refs)
    if not first:
        before_ref, ahead_ref = refs[:2]
        refs = refs[2:]
    before_out, send_ref = refs[:2]
    heads = own_ref.shape[0]
    base = packed_rows(heads)
    upper = is_upper(bit)
    weight = upper.astype(F32)

    def came_rows(at, count):
        return sums_got_ref[pl.ds(at, count), :].astype(F32)

    def left_rows(at, count):
        return jnp.where(upper, came_rows(at, count), sums_ref[pl.ds(at, count), :])

    lefts = unpack(left_rows, heads)
    cames = None if first else unpack(came_rows, heads)
    for h in range(heads):
        at = pl.ds(base + h * DH, DH)
        right = jnp.where(upper, sums_ref[at, :], sums_got_ref[at, :].astype(F32))
        got = got_ref[pl.ds(h * DH, DH), :].astype(F32)
        total = own_ref[h] + got + mm(lefts[h].astype(BF16), right.astype(BF16))
        if not last:
            refs[2][h] = total
        send_ref[pl.ds(h * DH, DH), :] = total.astype(BF16)
        if first:
            before_out[h] = weight * got
        else:
            product = mm(cames[h].astype(BF16), ahead_ref[at, :].astype(BF16))
            before_out[h] = before_ref[h] + weight * (got + product)


def union_pairs(bit, got, own, sums_got, sums, before, ahead, last):
    first = before is None
    return call(
        functools.partial(union_pairs_kernel, bit, first, last),
        vm(got, own, sums_got, sums) + ([] if first else vm(before, ahead)),
        [(own.shape, F32), (got.shape, BF16)] + ([] if last else [(own.shape, F32)]),
        flops=own.size * 4 * DH,
    )


def ahead_kernel(bit, got_ref, ahead_ref, before_ref, gram_ref, base_ref):
    weight = is_upper(bit).astype(F32)
    heads = before_ref.shape[0]
    base = packed_rows(heads)

    def came_rows(at, count):
        return got_ref[pl.ds(at, count), :].astype(F32)

    def ahead_rows(at, count):
        return ahead_ref[pl.ds(at, count), :] + weight * came_rows(at, count)

    cames = unpack(came_rows, heads)
    for h, gram in enumerate(unpack(ahead_rows, heads)):
        gram_ref[h] = gram.astype(BF16)
        cross = ahead_ref[pl.ds(base + h * DH, DH), :]
        base_ref[h] = before_ref[h] + weight * mm(cames[h].astype(BF16), cross.astype(BF16))


def ahead_of_device(bit, got, ahead, before):
    return call(
        functools.partial(ahead_kernel, bit),
        vm(got, ahead, before),
        [(before.shape, BF16), (before.shape, F32)],
        flops=before.size * 2 * DH,
    )


def inner_kernel(block, heads, q_ref, k_ref, v_ref, paired_ref, out_ref):
    rows = q_ref.shape[0]
    row, col = row_col(block)
    for n, h in enumerate(heads):
        for start in range(0, rows, block):
            at, end = pl.ds(start, block), start + block
            scores = mm_nt(q_ref[at, columns(h)], k_ref[pl.ds(0, end), columns(h)]).astype(BF16)
            result = None
            for first in range(0, end, block):
                upto = first + block
                mixing = mm(scores[:, :upto], paired_ref[h, pl.ds(0, upto), first:upto])
                if first == start:
                    mixing = jnp.where(row >= col, mixing, 0.0)
                more = mm(mixing.astype(BF16), v_ref[pl.ds(first, block), columns(h)])
                result = result + more if first else more
            out_ref[at, columns(n)] = result


def inner(q, k, v, paired, block, heads):
    rows = q.shape[0]
    return call(
        functools.partial(inner_kernel, block, heads),
        vm(q, k, v, paired),
        [((rows, len(heads) * DH), F32)],
        flops=rows * len(heads) * DH * 8 * block,
    )[0]


def outer_kernel(block, q_ref, v_ref, gram_ref, *refs):
    *part_refs, out_ref = refs
    rows = q_ref.shape[0]
    parts = [(ref, n) for ref in part_refs for n in range(ref.shape[1] // DH)]
    for h, (part_ref, n) in enumerate(parts):
        state = mm(q_ref[:, columns(h)], gram_ref[h]).astype(BF16)
        for start in range(0, rows, block):
            at, end = pl.ds(start, block), start + block
            row = lax.broadcasted_iota(jnp.int32, (block, end), 0) + start
            col = lax.broadcasted_iota(jnp.int32, (block, end), 1)
            mixing = mm_nt(state[start:end], q_ref[pl.ds(0, end), columns(h)])
            mixing = jnp.where(row >= col, mixing, 0.0).astype(BF16)
            out_ref[at, columns(h)] = part_ref[at, columns(n)] + mm(mixing, v_ref[pl.ds(0, end), columns(h)])


def outer(q, v, gram, parts, block):
    rows, width = q.shape
    return call(
        functools.partial(outer_kernel, block),
        vm(q, v, gram, *parts),
        [((rows, width), F32)],
        flops=rows * width * 6 * block,
    )[0]


def normed_kernel(bit, blocks, other, q_ref, part_ref, base_ref, got_ref, gain_ref, out_ref):
    weight = is_upper(bit).astype(F32)
    size = q_ref.shape[0] // blocks
    first = lax.bitwise_xor(lax.axis_index("head"), other)
    for h in range(base_ref.shape[0]):
        pair = (base_ref[h] + weight * got_ref[pl.ds(h * DH, DH), :].astype(F32)).astype(BF16)
        for j in range(blocks // 2):
            at = pl.ds(pl.multiple_of(lax.bitwise_xor(first, j) * size, size), size)
            attended = part_ref[at, columns(h)] + mm(q_ref[at, columns(h)], pair)
            mean = jnp.mean(attended * attended, axis=-1, keepdims=True)
            normed = attended * lax.rsqrt(mean + 1e-6) * gain_ref[:, columns(h)]
            out_ref[j, :, columns(h)] = normed.astype(BF16)


def normed_blocks(bit, other, q, part, base, got, gain, blocks):
    rows, width = q.shape
    return call(
        functools.partial(normed_kernel, bit, blocks, other),
        vm(q, part, base, got, gain),
        [((blocks // 2, rows // blocks, width), BF16)],
        flops=rows * width * DH,
    )[0]


def weights_kernel(shares, *refs):
    *parts, rest_ref, out_ref = refs
    sizes = [ref.shape[0] for ref in parts[:shares]]
    odd = lax.bitwise_and(lax.axis_index("seq"), 1)
    for n, size in enumerate(sizes):
        for first, ref in ((odd, parts[n]), (1 - odd, parts[shares + n])):
            at = pl.multiple_of(first * sum(sizes) + sum(sizes[:n]), 16)
            out_ref[pl.ds(at, size), :] = ref[...]
    out_ref[pl.ds(2 * sum(sizes), rest_ref.shape[0]), :] = rest_ref[...]


def join_weights(direct, neighbour, rest):
    rows = sum(part.shape[0] for part in (*direct, *neighbour, rest))
    return call(
        functools.partial(weights_kernel, len(direct)),
        vm(*direct, *neighbour, rest),
        [((rows, rest.shape[1]), BF16)],
        mib=8,
    )[0]


def project_own_kernel(kept_ref, w_ref, out_ref):
    blocks, size, width = kept_ref.shape
    kept = kept_ref[...].reshape(blocks * size, width)
    span = out_ref.shape[2]
    tile = 512 if span % 512 == 0 else span
    for start in range(0, span, tile):
        at = slice(start, start + tile)
        out_ref[:, :, at] = mm(kept, w_ref[:, at]).reshape(blocks, size, tile)


def project_own(kept, weight):
    blocks, size, width = kept.shape
    span = weight.shape[1]
    return call(
        project_own_kernel,
        vm(kept, weight),
        [((blocks, size, span), F32)],
        flops=2 * blocks * size * width * span,
        mib=8,
    )[0]


def project_kernel(index, own_ref, came_ref, w_ref, out_ref):
    span = out_ref.shape[1]
    tile = 512 if span % 512 == 0 else span
    for start in range(0, span, tile):
        at = slice(start, start + tile)
        out_ref[:, at] = (own_ref[index, :, at] + mm(came_ref[index], w_ref[:, at])).astype(out_ref.dtype)


def project(index, own, came, weight, dtype):
    _, size, span = own.shape
    return call(
        functools.partial(project_kernel, index),
        vm(own, came, weight),
        [((size, span), dtype)],
        flops=2 * size * came.shape[2] * span,
        mib=8,
    )[0]


def flip(value, axis, bit):
    count = lax.axis_size(axis)
    return lax.ppermute(value, axis, [(i, i ^ bit) for i in range(count)])


def shards(queries, key_vectors, value_vectors, norm_gain, out_weight):
    rows, width = queries.shape
    seq_count, head_count = lax.axis_size("seq"), lax.axis_size("head")
    block = 256 if rows % 256 == 0 else rows

    top = head_count // 2
    features = out_weight.shape[0]
    sizes = [features * n // 32 // 16 * 16 for n in SHARES]

    q, k, v, sums, sums_send, *weight_shares = local_sums(
        queries, key_vectors, value_vectors, out_weight, sizes
    )
    pairs, pairs_send, paired, weight_rest = local_pairs(
        q, k, v, out_weight, features - 2 * sum(sizes), block
    )
    direct = [flip(w, "head", top) for w in weight_shares]
    neighbour = [flip(w, "seq", 1) for w in direct]
    rest = flip(weight_rest, "head", top)
    heads = width // DH
    parts = [
        inner(q, k, v, paired, block, tuple(range(at, min(at + (heads + 1) // 2, heads))))
        for at in range(0, heads, (heads + 1) // 2)
    ]
    ahead = before = None
    bit = 1
    while 2 * bit < seq_count:
        sums_got = flip(sums_send, "seq", bit)
        pairs_got = flip(pairs_send, "seq", bit)
        last = 4 * bit >= seq_count
        old = ahead
        ahead, sums_send, *more_sums = union_sums(bit, sums_got, sums, ahead, heads, last)
        before, pairs_send, *more_pairs = union_pairs(
            bit, pairs_got, pairs, sums_got, sums, before, old, last
        )
        if not last:
            (pairs,), (sums,) = more_pairs, more_sums
        bit *= 2
    gram_got = flip(sums_send, "seq", bit)
    pairs_got = flip(pairs_send, "seq", bit)
    gram, base = ahead_of_device(bit, gram_got, ahead, before)
    part = outer(q, v, gram, parts, block)

    gain = norm_gain.reshape(1, width)
    sent = normed_blocks(bit, top, q, part, base, pairs_got, gain, head_count)
    came = flip(sent, "head", top)
    kept = normed_blocks(bit, 0, q, part, base, pairs_got, gain, head_count)
    own = project_own(kept, out_weight)
    weight_came = join_weights(direct, neighbour, rest)

    count = top
    if count == 1:
        return project(0, own, came, weight_came, BF16)
    results = {
        j: project(j, own, came, weight_came, BF16 if 2 * j >= count else F32) for j in reversed(range(count))
    }
    while count > 1:
        count //= 2
        for j in range(count):
            got = flip(results[count + j].astype(BF16), "head", count)
            results[j] = results[j].astype(F32) + got.astype(F32)
    return results[0].astype(BF16)


def solution(mesh):
    in_specs = (P("seq", "head"), P("seq", "head"), P("seq", "head"), P("head"), P("head", None))
    out_specs = P(("seq", "head"), None)

    return jax.shard_map(shards, mesh=mesh, in_specs=in_specs, out_specs=out_specs, check_vma=False)
```

```python
import functools

import jax
import jax.numpy as jnp
from jax import lax
from jax.experimental import pallas as pl
from jax.experimental.pallas import tpu as pltpu
from jax.sharding import PartitionSpec as P


DH = 128
DIAG = 16
SHARES = (5, 5, 4)
F32 = jnp.float32
BF16 = jnp.bfloat16


def mm(a, b):
    return lax.dot_general(a, b, (((1,), (0,)), ((), ())), preferred_element_type=F32)


def mm_nt(a, b):
    return lax.dot_general(a, b, (((1,), (1,)), ((), ())), preferred_element_type=F32)


def mm_tn(a, b):
    return lax.dot_general(a, b, (((0,), (0,)), ((), ())), preferred_element_type=F32)


def row_col(n):
    return lax.broadcasted_iota(jnp.int32, (n, n), 0), lax.broadcasted_iota(jnp.int32, (n, n), 1)


def is_upper(bit):
    return lax.bitwise_and(lax.axis_index("seq"), bit) != 0


def columns(h):
    return slice(h * DH, (h + 1) * DH)


def call(kernel, ins, outs, flops=0, scratch=(), mib=4):
    arrays = [pltpu.with_memory_space_constraint(a, space) if space is pltpu.HBM else a for a, space in ins]
    data = sum(a.size * a.dtype.itemsize for a in arrays)
    return pl.pallas_call(
        kernel,
        in_specs=[pl.BlockSpec(memory_space=space) for a, space in ins],
        out_specs=[pl.BlockSpec(memory_space=pltpu.VMEM) for o in outs],
        out_shape=[pltpu.VMEM(shape, dtype) for shape, dtype in outs],
        scratch_shapes=list(scratch),
        compiler_params=pltpu.CompilerParams(vmem_limit_bytes=mib << 20),
        cost_estimate=pl.CostEstimate(flops=int(flops), bytes_accessed=int(data), transcendentals=0),
    )(*arrays)


def vm(*arrays):
    return [(a, pltpu.VMEM) for a in arrays]


def pack(grams):
    heads = len(grams)
    row, col = row_col(DH)
    parts, diagonals = [], []
    for p in range(0, heads, 2):
        a, b = grams[p], grams[min(p + 1, heads - 1)]
        parts.append(jnp.where(row <= col, a, b))
        diagonals.append(jnp.sum(jnp.where(row == col, b, 0.0), axis=0, keepdims=True))
    diagonals += [jnp.zeros((1, DH), F32)] * (DIAG - len(diagonals))
    return parts, jnp.concatenate(diagonals, axis=0)


def unpack(rows_of, heads):
    pairs = (heads + 1) // 2
    row, col = row_col(DH)
    diagonals = rows_of(pairs * DH, DIAG)
    grams = []
    for p in range(pairs):
        m = rows_of(p * DH, DH)
        t = m.T
        d = jnp.broadcast_to(diagonals[p : p + 1, :], (DH, DH))
        grams.append(jnp.where(row <= col, m, t))
        grams.append(jnp.where(row > col, m, jnp.where(row < col, t, d)))
    return grams[:heads]


def packed_rows(heads):
    return (heads + 1) // 2 * DH + DIAG


def sums_kernel(chunks, q_hbm, k_hbm, v_hbm, w_hbm, q_ref, k_ref, v_ref, own_ref, send_ref, *refs):
    *w_refs, sem, w_sem = refs
    rows, width = q_ref.shape
    heads = width // DH
    size = rows // chunks
    copies = []
    for c in range(chunks):
        at = pl.ds(c * size, size)
        for n, (src, dst) in enumerate(((k_hbm, k_ref), (q_hbm, q_ref), (v_hbm, v_ref))):
            copies.append(pltpu.make_async_copy(src.at[at], dst.at[at], sem.at[c, n]))
    sizes = [ref.shape[0] for ref in w_refs]
    first = lax.bitwise_and(lax.axis_index("seq"), 1) * sum(sizes)
    for n, w_ref in enumerate(w_refs):
        at = pl.multiple_of(first + sum(sizes[:n]), 16)
        copies.append(pltpu.make_async_copy(w_hbm.at[pl.ds(at, sizes[n])], w_ref, w_sem.at[n]))
    for copy in copies:
        copy.start()
    grams = [None] * heads
    crosses = [None] * heads
    for c in range(chunks):
        at = pl.ds(c * size, size)
        copies[3 * c].wait()
        for h in range(heads):
            k = k_ref[at, columns(h)]
            gram = mm_tn(k, k)
            grams[h] = gram if c == 0 else grams[h] + gram
        copies[3 * c + 1].wait()
        copies[3 * c + 2].wait()
        for h in range(heads):
            cross = mm_tn(q_ref[at, columns(h)], v_ref[at, columns(h)])
            crosses[h] = cross if c == 0 else crosses[h] + cross
    parts, diagonals = pack(grams)
    base = packed_rows(heads)
    places = [(p * DH, part) for p, part in enumerate(parts)] + [(base - DIAG, diagonals)]
    for at, part in places + [(base + h * DH, cross) for h, cross in enumerate(crosses)]:
        own_ref[pl.ds(at, part.shape[0]), :] = part
        send_ref[pl.ds(at, part.shape[0]), :] = part.astype(BF16)
    for copy in copies[3 * chunks :]:
        copy.wait()


def local_sums(q, k, v, weight, sizes):
    rows, width = q.shape
    heads = width // DH
    chunks = 1
    return call(
        functools.partial(sums_kernel, chunks),
        [(a, pltpu.HBM) for a in (q, k, v, weight)],
        [((rows, width), BF16)] * 3
        + [((packed_rows(heads) + heads * DH, DH), dtype) for dtype in (F32, BF16)]
        + [((size, weight.shape[1]), BF16) for size in sizes],
        flops=4 * rows * width * DH,
        scratch=[pltpu.SemaphoreType.DMA((chunks, 3)), pltpu.SemaphoreType.DMA((len(sizes),))],
        mib=6,
    )


def pairs_kernel(block, q_ref, k_ref, v_ref, w_hbm, own_ref, send_ref, paired_ref, w_ref, w_sem):
    rest = w_ref.shape[0]
    copy = pltpu.make_async_copy(w_hbm.at[pl.ds(w_hbm.shape[0] - rest, rest)], w_ref, w_sem)
    copy.start()
    rows, width = q_ref.shape
    for h in range(width // DH):
        pair = None
        for start in range(0, rows, block):
            span = rows - start
            at, on = pl.ds(start, block), pl.ds(start, span)
            k = k_ref[at, columns(h)]
            row = lax.broadcasted_iota(jnp.int32, (block, span), 0)
            col = lax.broadcasted_iota(jnp.int32, (block, span), 1)
            paired = jnp.where(row < col, mm_nt(k, q_ref[on, columns(h)]), 0.0).astype(BF16)
            paired_ref[h, at, start:rows] = paired
            here = mm_tn(k, mm(paired, v_ref[on, columns(h)]).astype(BF16))
            pair = pair + here if start else here
        own_ref[h] = pair
        send_ref[pl.ds(h * DH, DH), :] = pair.astype(BF16)
    copy.wait()


def local_pairs(q, k, v, weight, rest, block):
    rows, width = q.shape
    heads = width // DH
    return call(
        functools.partial(pairs_kernel, block),
        vm(q, k, v) + [(weight, pltpu.HBM)],
        [
            ((heads, DH, DH), F32),
            ((heads * DH, DH), BF16),
            ((heads, rows, rows), BF16),
            ((rest, weight.shape[1]), BF16),
        ],
        flops=4 * rows * width * block,
        scratch=[pltpu.SemaphoreType.DMA],
        mib=8,
    )


def union_sums_kernel(bit, first, last, got_ref, own_ref, *refs):
    refs = list(refs)
    ahead_ref = None if first else refs.pop(0)
    ahead_out, send_ref = refs[:2]
    got = got_ref[...].astype(F32)
    total = own_ref[...] + got
    sent = send_ref.shape[0]
    send_ref[...] = total[:sent].astype(BF16)
    if not last:
        refs[2][...] = total
    ahead = is_upper(bit).astype(F32) * got
    ahead_out[...] = ahead if first else ahead_ref[...] + ahead


def union_sums(bit, got, own, ahead, heads, last):
    first = ahead is None
    sent = packed_rows(heads) if last else got.shape[0]
    return call(
        functools.partial(union_sums_kernel, bit, first, last),
        vm(got, own) + ([] if first else vm(ahead)),
        [(own.shape, F32), ((sent, DH), BF16)] + ([] if last else [(own.shape, F32)]),
    )


def union_pairs_kernel(bit, first, last, got_ref, own_ref, sums_got_ref, sums_ref, *refs):
    refs = list(refs)
    if not first:
        before_ref, ahead_ref = refs[:2]
        refs = refs[2:]
    before_out, send_ref = refs[:2]
    heads = own_ref.shape[0]
    base = packed_rows(heads)
    upper = is_upper(bit)
    weight = upper.astype(F32)

    def came_rows(at, count):
        return sums_got_ref[pl.ds(at, count), :].astype(F32)

    def left_rows(at, count):
        return jnp.where(upper, came_rows(at, count), sums_ref[pl.ds(at, count), :])

    lefts = unpack(left_rows, heads)
    cames = None if first else unpack(came_rows, heads)
    for h in range(heads):
        at = pl.ds(base + h * DH, DH)
        right = jnp.where(upper, sums_ref[at, :], sums_got_ref[at, :].astype(F32))
        got = got_ref[pl.ds(h * DH, DH), :].astype(F32)
        total = own_ref[h] + got + mm(lefts[h].astype(BF16), right.astype(BF16))
        if not last:
            refs[2][h] = total
        send_ref[pl.ds(h * DH, DH), :] = total.astype(BF16)
        if first:
            before_out[h] = weight * got
        else:
            product = mm(cames[h].astype(BF16), ahead_ref[at, :].astype(BF16))
            before_out[h] = before_ref[h] + weight * (got + product)


def union_pairs(bit, got, own, sums_got, sums, before, ahead, last):
    first = before is None
    return call(
        functools.partial(union_pairs_kernel, bit, first, last),
        vm(got, own, sums_got, sums) + ([] if first else vm(before, ahead)),
        [(own.shape, F32), (got.shape, BF16)] + ([] if last else [(own.shape, F32)]),
        flops=own.size * 4 * DH,
    )


def ahead_kernel(bit, got_ref, ahead_ref, before_ref, gram_ref, base_ref):
    weight = is_upper(bit).astype(F32)
    heads = before_ref.shape[0]
    base = packed_rows(heads)

    def came_rows(at, count):
        return got_ref[pl.ds(at, count), :].astype(F32)

    def ahead_rows(at, count):
        return ahead_ref[pl.ds(at, count), :] + weight * came_rows(at, count)

    cames = unpack(came_rows, heads)
    for h, gram in enumerate(unpack(ahead_rows, heads)):
        gram_ref[h] = gram.astype(BF16)
        cross = ahead_ref[pl.ds(base + h * DH, DH), :]
        base_ref[h] = before_ref[h] + weight * mm(cames[h].astype(BF16), cross.astype(BF16))


def ahead_of_device(bit, got, ahead, before):
    return call(
        functools.partial(ahead_kernel, bit),
        vm(got, ahead, before),
        [(before.shape, BF16), (before.shape, F32)],
        flops=before.size * 2 * DH,
    )


def inner_kernel(block, heads, q_ref, k_ref, v_ref, paired_ref, out_ref):
    rows = q_ref.shape[0]
    row, col = row_col(block)
    for n, h in enumerate(heads):
        for start in range(0, rows, block):
            at, end = pl.ds(start, block), start + block
            scores = mm_nt(q_ref[at, columns(h)], k_ref[pl.ds(0, end), columns(h)]).astype(BF16)
            result = None
            for first in range(0, end, block):
                upto = first + block
                mixing = mm(scores[:, :upto], paired_ref[h, pl.ds(0, upto), first:upto])
                if first == start:
                    mixing = jnp.where(row >= col, mixing, 0.0)
                more = mm(mixing.astype(BF16), v_ref[pl.ds(first, block), columns(h)])
                result = result + more if first else more
            out_ref[at, columns(n)] = result


def inner(q, k, v, paired, block, heads):
    rows = q.shape[0]
    return call(
        functools.partial(inner_kernel, block, heads),
        vm(q, k, v, paired),
        [((rows, len(heads) * DH), F32)],
        flops=rows * len(heads) * DH * 8 * block,
    )[0]


def outer_kernel(block, q_ref, v_ref, gram_ref, *refs):
    *part_refs, out_ref = refs
    rows = q_ref.shape[0]
    parts = [(ref, n) for ref in part_refs for n in range(ref.shape[1] // DH)]
    for h, (part_ref, n) in enumerate(parts):
        state = mm(q_ref[:, columns(h)], gram_ref[h]).astype(BF16)
        for start in range(0, rows, block):
            at, end = pl.ds(start, block), start + block
            row = lax.broadcasted_iota(jnp.int32, (block, end), 0) + start
            col = lax.broadcasted_iota(jnp.int32, (block, end), 1)
            mixing = mm_nt(state[start:end], q_ref[pl.ds(0, end), columns(h)])
            mixing = jnp.where(row >= col, mixing, 0.0).astype(BF16)
            out_ref[at, columns(h)] = part_ref[at, columns(n)] + mm(mixing, v_ref[pl.ds(0, end), columns(h)])


def outer(q, v, gram, parts, block):
    rows, width = q.shape
    return call(
        functools.partial(outer_kernel, block),
        vm(q, v, gram, *parts),
        [((rows, width), F32)],
        flops=rows * width * 6 * block,
    )[0]


def normed_kernel(bit, blocks, other, q_ref, part_ref, base_ref, got_ref, gain_ref, *out_refs):
    weight = is_upper(bit).astype(F32)
    size = q_ref.shape[0] // blocks
    first = lax.bitwise_xor(lax.axis_index("head"), other)
    for h in range(base_ref.shape[0]):
        pair = (base_ref[h] + weight * got_ref[pl.ds(h * DH, DH), :].astype(F32)).astype(BF16)
        for j in range(blocks // 2):
            at = pl.ds(pl.multiple_of(lax.bitwise_xor(first, j) * size, size), size)
            attended = part_ref[at, columns(h)] + mm(q_ref[at, columns(h)], pair)
            mean = jnp.mean(attended * attended, axis=-1, keepdims=True)
            normed = attended * lax.rsqrt(mean + 1e-6) * gain_ref[:, columns(h)]
            out_refs[j][:, columns(h)] = normed.astype(BF16)


def normed_blocks(bit, other, q, part, base, got, gain, blocks):
    rows, width = q.shape
    return call(
        functools.partial(normed_kernel, bit, blocks, other),
        vm(q, part, base, got, gain),
        [((rows // blocks, width), BF16)] * (blocks // 2),
        flops=rows * width * DH,
    )


def weights_kernel(shares, *refs):
    *parts, rest_ref, out_ref = refs
    sizes = [ref.shape[0] for ref in parts[:shares]]
    odd = lax.bitwise_and(lax.axis_index("seq"), 1)
    for n, size in enumerate(sizes):
        for first, ref in ((odd, parts[n]), (1 - odd, parts[shares + n])):
            at = pl.multiple_of(first * sum(sizes) + sum(sizes[:n]), 16)
            out_ref[pl.ds(at, size), :] = ref[...]
    out_ref[pl.ds(2 * sum(sizes), rest_ref.shape[0]), :] = rest_ref[...]


def join_weights(direct, neighbour, rest):
    rows = sum(part.shape[0] for part in (*direct, *neighbour, rest))
    return call(
        functools.partial(weights_kernel, len(direct)),
        vm(*direct, *neighbour, rest),
        [((rows, rest.shape[1]), BF16)],
        mib=8,
    )[0]


def project_own_kernel(w_ref, *refs):
    count = len(refs) // 2
    span = w_ref.shape[1]
    tile = 512 if span % 512 == 0 else span
    kept = jnp.concatenate([ref[...] for ref in refs[:count]], axis=0)
    size = kept.shape[0] // count
    for start in range(0, span, tile):
        at = slice(start, start + tile)
        total = mm(kept, w_ref[:, at])
        for n, out_ref in enumerate(refs[count:]):
            out_ref[:, at] = total[n * size : (n + 1) * size]


def project_own(kept, weight):
    size, width = kept[0].shape
    span = weight.shape[1]
    return call(
        project_own_kernel,
        vm(weight, *kept),
        [((size, span), F32)] * len(kept),
        flops=2 * len(kept) * size * width * span,
        mib=8,
    )


def project_kernel(own_ref, came_ref, w_ref, out_ref):
    span = out_ref.shape[1]
    tile = 512 if span % 512 == 0 else span
    for start in range(0, span, tile):
        at = slice(start, start + tile)
        out_ref[:, at] = (own_ref[:, at] + mm(came_ref[...], w_ref[:, at])).astype(out_ref.dtype)


def project(own, came, weight, dtype):
    size, span = own.shape
    return call(
        project_kernel,
        vm(own, came, weight),
        [((size, span), dtype)],
        flops=2 * size * came.shape[1] * span,
        mib=8,
    )[0]


def flip(value, axis, bit):
    count = lax.axis_size(axis)
    return lax.ppermute(value, axis, [(i, i ^ bit) for i in range(count)])


def shards(queries, key_vectors, value_vectors, norm_gain, out_weight):
    rows, width = queries.shape
    seq_count, head_count = lax.axis_size("seq"), lax.axis_size("head")
    block = 256 if rows % 256 == 0 else rows

    top = head_count // 2
    features = out_weight.shape[0]
    sizes = [features * n // 32 // 16 * 16 for n in SHARES]

    q, k, v, sums, sums_send, *weight_shares = local_sums(
        queries, key_vectors, value_vectors, out_weight, sizes
    )
    pairs, pairs_send, paired, weight_rest = local_pairs(
        q, k, v, out_weight, features - 2 * sum(sizes), block
    )
    direct = [flip(w, "head", top) for w in weight_shares]
    neighbour = [flip(w, "seq", 1) for w in direct]
    rest = flip(weight_rest, "head", top)
    heads = width // DH
    parts = [
        inner(q, k, v, paired, block, tuple(range(at, min(at + (heads + 1) // 2, heads))))
        for at in range(0, heads, (heads + 1) // 2)
    ]
    ahead = before = None
    bit = 1
    while 2 * bit < seq_count:
        sums_got = flip(sums_send, "seq", bit)
        pairs_got = flip(pairs_send, "seq", bit)
        last = 4 * bit >= seq_count
        old = ahead
        ahead, sums_send, *more_sums = union_sums(bit, sums_got, sums, ahead, heads, last)
        before, pairs_send, *more_pairs = union_pairs(
            bit, pairs_got, pairs, sums_got, sums, before, old, last
        )
        if not last:
            (pairs,), (sums,) = more_pairs, more_sums
        bit *= 2
    gram_got = flip(sums_send, "seq", bit)
    pairs_got = flip(pairs_send, "seq", bit)
    gram, base = ahead_of_device(bit, gram_got, ahead, before)
    part = outer(q, v, gram, parts, block)

    gain = norm_gain.reshape(1, width)
    sent = normed_blocks(bit, top, q, part, base, pairs_got, gain, head_count)
    came = [flip(rows_sent, "head", top) for rows_sent in sent]
    kept = normed_blocks(bit, 0, q, part, base, pairs_got, gain, head_count)
    own = project_own(kept, out_weight)
    weight_came = join_weights(direct, neighbour, rest)

    count = top
    results = {
        j: project(own[j], came[j], weight_came, BF16 if 2 * j >= count else F32)
        for j in reversed(range(count))
    }
    while count > 1:
        count //= 2
        for j in range(count):
            got = flip(results[count + j].astype(BF16), "head", count)
            results[j] = results[j].astype(F32) + got.astype(F32)
    return results[0].astype(BF16)


def solution(mesh):
    in_specs = (P("seq", "head"), P("seq", "head"), P("seq", "head"), P("head"), P("head", None))
    out_specs = P(("seq", "head"), None)

    return jax.shard_map(shards, mesh=mesh, in_specs=in_specs, out_specs=out_specs, check_vma=False)
```

```python
import functools

import jax
import jax.numpy as jnp
from jax import lax
from jax.experimental import pallas as pl
from jax.experimental.pallas import tpu as pltpu
from jax.sharding import PartitionSpec as P


DH = 128
DIAG = 16
SHARES = ((6, 1), (6, 1), (2, 2))
F32 = jnp.float32
BF16 = jnp.bfloat16


def mm(a, b):
    return lax.dot_general(a, b, (((1,), (0,)), ((), ())), preferred_element_type=F32)


def mm_nt(a, b):
    return lax.dot_general(a, b, (((1,), (1,)), ((), ())), preferred_element_type=F32)


def mm_tn(a, b):
    return lax.dot_general(a, b, (((0,), (0,)), ((), ())), preferred_element_type=F32)


def row_col(n):
    return lax.broadcasted_iota(jnp.int32, (n, n), 0), lax.broadcasted_iota(jnp.int32, (n, n), 1)


def is_upper(bit):
    return lax.bitwise_and(lax.axis_index("seq"), bit) != 0


def columns(h):
    return slice(h * DH, (h + 1) * DH)


def call(kernel, ins, outs, flops=0, scratch=(), mib=4):
    arrays = [pltpu.with_memory_space_constraint(a, space) if space is pltpu.HBM else a for a, space in ins]
    data = sum(a.size * a.dtype.itemsize for a in arrays)
    return pl.pallas_call(
        kernel,
        in_specs=[pl.BlockSpec(memory_space=space) for a, space in ins],
        out_specs=[pl.BlockSpec(memory_space=pltpu.VMEM) for o in outs],
        out_shape=[pltpu.VMEM(shape, dtype) for shape, dtype in outs],
        scratch_shapes=list(scratch),
        compiler_params=pltpu.CompilerParams(vmem_limit_bytes=mib << 20),
        cost_estimate=pl.CostEstimate(flops=int(flops), bytes_accessed=int(data), transcendentals=0),
    )(*arrays)


def vm(*arrays):
    return [(a, pltpu.VMEM) for a in arrays]


def pack(grams):
    heads = len(grams)
    row, col = row_col(DH)
    parts, diagonals = [], []
    for p in range(0, heads, 2):
        a, b = grams[p], grams[min(p + 1, heads - 1)]
        parts.append(jnp.where(row <= col, a, b))
        diagonals.append(jnp.sum(jnp.where(row == col, b, 0.0), axis=0, keepdims=True))
    diagonals += [jnp.zeros((1, DH), F32)] * (DIAG - len(diagonals))
    return parts, jnp.concatenate(diagonals, axis=0)


def unpack(rows_of, heads):
    pairs = (heads + 1) // 2
    row, col = row_col(DH)
    diagonals = rows_of(pairs * DH, DIAG)
    grams = []
    for p in range(pairs):
        m = rows_of(p * DH, DH)
        t = m.T
        d = jnp.broadcast_to(diagonals[p : p + 1, :], (DH, DH))
        grams.append(jnp.where(row <= col, m, t))
        grams.append(jnp.where(row > col, m, jnp.where(row < col, t, d)))
    return grams[:heads]


def packed_rows(heads):
    return (heads + 1) // 2 * DH + DIAG


def share_places(sizes, bits):
    places, at = [], 0
    for bit in sorted(set(bits)):
        region = sum(size for size, b in zip(sizes, bits) if b == bit)
        skip = 0
        for n, size in enumerate(sizes):
            if bits[n] == bit:
                places.append((n, (bit, at + skip, at + region + skip)))
                skip += size
        at += 2 * region
    return [place for n, place in sorted(places)]


def share_row(bit, low, high, other=False):
    upper = is_upper(bit)
    if other:
        upper = jnp.logical_not(upper)
    return pl.multiple_of(jnp.where(upper, high, low), 16)


def sums_kernel(chunks, places, q_hbm, k_hbm, v_hbm, w_hbm, q_ref, k_ref, v_ref, own_ref, send_ref, *refs):
    *w_refs, sem, w_sem = refs
    rows, width = q_ref.shape
    heads = width // DH
    size = rows // chunks
    copies = []
    for c in range(chunks):
        at = pl.ds(c * size, size)
        for n, (src, dst) in enumerate(((k_hbm, k_ref), (q_hbm, q_ref), (v_hbm, v_ref))):
            copies.append(pltpu.make_async_copy(src.at[at], dst.at[at], sem.at[c, n]))
    for n, (w_ref, (bit, low, high)) in enumerate(zip(w_refs, places)):
        at = share_row(bit, low, high)
        copies.append(pltpu.make_async_copy(w_hbm.at[pl.ds(at, w_ref.shape[0])], w_ref, w_sem.at[n]))
    for copy in copies:
        copy.start()
    grams = [None] * heads
    crosses = [None] * heads
    for c in range(chunks):
        at = pl.ds(c * size, size)
        copies[3 * c].wait()
        for h in range(heads):
            k = k_ref[at, columns(h)]
            gram = mm_tn(k, k)
            grams[h] = gram if c == 0 else grams[h] + gram
        copies[3 * c + 1].wait()
        copies[3 * c + 2].wait()
        for h in range(heads):
            cross = mm_tn(q_ref[at, columns(h)], v_ref[at, columns(h)])
            crosses[h] = cross if c == 0 else crosses[h] + cross
    parts, diagonals = pack(grams)
    base = packed_rows(heads)
    places = [(p * DH, part) for p, part in enumerate(parts)] + [(base - DIAG, diagonals)]
    for at, part in places + [(base + h * DH, cross) for h, cross in enumerate(crosses)]:
        own_ref[pl.ds(at, part.shape[0]), :] = part
        send_ref[pl.ds(at, part.shape[0]), :] = part.astype(BF16)
    for copy in copies[3 * chunks :]:
        copy.wait()


def local_sums(q, k, v, weight, sizes, places):
    rows, width = q.shape
    heads = width // DH
    chunks = 1
    return call(
        functools.partial(sums_kernel, chunks, places),
        [(a, pltpu.HBM) for a in (q, k, v, weight)],
        [((rows, width), BF16)] * 3
        + [((packed_rows(heads) + heads * DH, DH), dtype) for dtype in (F32, BF16)]
        + [((size, weight.shape[1]), BF16) for size in sizes],
        flops=4 * rows * width * DH,
        scratch=[pltpu.SemaphoreType.DMA((chunks, 3)), pltpu.SemaphoreType.DMA((len(sizes),))],
        mib=6,
    )


def pairs_kernel(block, q_ref, k_ref, v_ref, w_hbm, own_ref, send_ref, paired_ref, w_ref, w_sem):
    rest = w_ref.shape[0]
    copy = pltpu.make_async_copy(w_hbm.at[pl.ds(w_hbm.shape[0] - rest, rest)], w_ref, w_sem)
    copy.start()
    rows, width = q_ref.shape
    for h in range(width // DH):
        pair = None
        for start in range(0, rows, block):
            span = rows - start
            at, on = pl.ds(start, block), pl.ds(start, span)
            k = k_ref[at, columns(h)]
            row = lax.broadcasted_iota(jnp.int32, (block, span), 0)
            col = lax.broadcasted_iota(jnp.int32, (block, span), 1)
            paired = jnp.where(row < col, mm_nt(k, q_ref[on, columns(h)]), 0.0).astype(BF16)
            paired_ref[h, at, start:rows] = paired
            here = mm_tn(k, mm(paired, v_ref[on, columns(h)]).astype(BF16))
            pair = pair + here if start else here
        own_ref[h] = pair
        send_ref[pl.ds(h * DH, DH), :] = pair.astype(BF16)
    copy.wait()


def local_pairs(q, k, v, weight, rest, block):
    rows, width = q.shape
    heads = width // DH
    return call(
        functools.partial(pairs_kernel, block),
        vm(q, k, v) + [(weight, pltpu.HBM)],
        [
            ((heads, DH, DH), F32),
            ((heads * DH, DH), BF16),
            ((heads, rows, rows), BF16),
            ((rest, weight.shape[1]), BF16),
        ],
        flops=4 * rows * width * block,
        scratch=[pltpu.SemaphoreType.DMA],
        mib=8,
    )


def union_sums_kernel(bit, first, last, got_ref, own_ref, *refs):
    refs = list(refs)
    ahead_ref = None if first else refs.pop(0)
    ahead_out, send_ref = refs[:2]
    got = got_ref[...].astype(F32)
    total = own_ref[...] + got
    sent = send_ref.shape[0]
    send_ref[...] = total[:sent].astype(BF16)
    if not last:
        refs[2][...] = total
    ahead = is_upper(bit).astype(F32) * got
    ahead_out[...] = ahead if first else ahead_ref[...] + ahead


def union_sums(bit, got, own, ahead, heads, last):
    first = ahead is None
    sent = packed_rows(heads) if last else got.shape[0]
    return call(
        functools.partial(union_sums_kernel, bit, first, last),
        vm(got, own) + ([] if first else vm(ahead)),
        [(own.shape, F32), ((sent, DH), BF16)] + ([] if last else [(own.shape, F32)]),
    )


def union_pairs_kernel(bit, first, last, got_ref, own_ref, sums_got_ref, sums_ref, *refs):
    refs = list(refs)
    if not first:
        before_ref, ahead_ref = refs[:2]
        refs = refs[2:]
    before_out, send_ref = refs[:2]
    heads = own_ref.shape[0]
    base = packed_rows(heads)
    upper = is_upper(bit)
    weight = upper.astype(F32)

    def came_rows(at, count):
        return sums_got_ref[pl.ds(at, count), :].astype(F32)

    def left_rows(at, count):
        return jnp.where(upper, came_rows(at, count), sums_ref[pl.ds(at, count), :])

    lefts = unpack(left_rows, heads)
    cames = None if first else unpack(came_rows, heads)
    for h in range(heads):
        at = pl.ds(base + h * DH, DH)
        right = jnp.where(upper, sums_ref[at, :], sums_got_ref[at, :].astype(F32))
        got = got_ref[pl.ds(h * DH, DH), :].astype(F32)
        total = own_ref[h] + got + mm(lefts[h].astype(BF16), right.astype(BF16))
        if not last:
            refs[2][h] = total
        send_ref[pl.ds(h * DH, DH), :] = total.astype(BF16)
        if first:
            before_out[h] = weight * got
        else:
            product = mm(cames[h].astype(BF16), ahead_ref[at, :].astype(BF16))
            before_out[h] = before_ref[h] + weight * (got + product)


def union_pairs(bit, got, own, sums_got, sums, before, ahead, last):
    first = before is None
    return call(
        functools.partial(union_pairs_kernel, bit, first, last),
        vm(got, own, sums_got, sums) + ([] if first else vm(before, ahead)),
        [(own.shape, F32), (got.shape, BF16)] + ([] if last else [(own.shape, F32)]),
        flops=own.size * 4 * DH,
    )


def ahead_kernel(bit, got_ref, ahead_ref, before_ref, gram_ref, base_ref):
    weight = is_upper(bit).astype(F32)
    heads = before_ref.shape[0]
    base = packed_rows(heads)

    def came_rows(at, count):
        return got_ref[pl.ds(at, count), :].astype(F32)

    def ahead_rows(at, count):
        return ahead_ref[pl.ds(at, count), :] + weight * came_rows(at, count)

    cames = unpack(came_rows, heads)
    for h, gram in enumerate(unpack(ahead_rows, heads)):
        gram_ref[h] = gram.astype(BF16)
        cross = ahead_ref[pl.ds(base + h * DH, DH), :]
        base_ref[h] = before_ref[h] + weight * mm(cames[h].astype(BF16), cross.astype(BF16))


def ahead_of_device(bit, got, ahead, before):
    return call(
        functools.partial(ahead_kernel, bit),
        vm(got, ahead, before),
        [(before.shape, BF16), (before.shape, F32)],
        flops=before.size * 2 * DH,
    )


def inner_kernel(block, heads, q_ref, k_ref, v_ref, paired_ref, out_ref):
    rows = q_ref.shape[0]
    row, col = row_col(block)
    for n, h in enumerate(heads):
        for start in range(0, rows, block):
            at, end = pl.ds(start, block), start + block
            scores = mm_nt(q_ref[at, columns(h)], k_ref[pl.ds(0, end), columns(h)]).astype(BF16)
            result = None
            for first in range(0, end, block):
                upto = first + block
                mixing = mm(scores[:, :upto], paired_ref[h, pl.ds(0, upto), first:upto])
                if first == start:
                    mixing = jnp.where(row >= col, mixing, 0.0)
                more = mm(mixing.astype(BF16), v_ref[pl.ds(first, block), columns(h)])
                result = result + more if first else more
            out_ref[at, columns(n)] = result


def inner(q, k, v, paired, block, heads):
    rows = q.shape[0]
    return call(
        functools.partial(inner_kernel, block, heads),
        vm(q, k, v, paired),
        [((rows, len(heads) * DH), F32)],
        flops=rows * len(heads) * DH * 8 * block,
    )[0]


def outer_kernel(block, q_ref, v_ref, gram_ref, *refs):
    *part_refs, out_ref = refs
    rows = q_ref.shape[0]
    parts = [(ref, n) for ref in part_refs for n in range(ref.shape[1] // DH)]
    for h, (part_ref, n) in enumerate(parts):
        state = mm(q_ref[:, columns(h)], gram_ref[h]).astype(BF16)
        for start in range(0, rows, block):
            at, end = pl.ds(start, block), start + block
            row = lax.broadcasted_iota(jnp.int32, (block, end), 0) + start
            col = lax.broadcasted_iota(jnp.int32, (block, end), 1)
            mixing = mm_nt(state[start:end], q_ref[pl.ds(0, end), columns(h)])
            mixing = jnp.where(row >= col, mixing, 0.0).astype(BF16)
            out_ref[at, columns(h)] = part_ref[at, columns(n)] + mm(mixing, v_ref[pl.ds(0, end), columns(h)])


def outer(q, v, gram, parts, block):
    rows, width = q.shape
    return call(
        functools.partial(outer_kernel, block),
        vm(q, v, gram, *parts),
        [((rows, width), F32)],
        flops=rows * width * 6 * block,
    )[0]


def normed_kernel(bit, blocks, other, q_ref, part_ref, base_ref, got_ref, gain_ref, *out_refs):
    weight = is_upper(bit).astype(F32)
    size = q_ref.shape[0] // blocks
    first = lax.bitwise_xor(lax.axis_index("head"), other)
    for h in range(base_ref.shape[0]):
        pair = (base_ref[h] + weight * got_ref[pl.ds(h * DH, DH), :].astype(F32)).astype(BF16)
        for j in range(blocks // 2):
            at = pl.ds(pl.multiple_of(lax.bitwise_xor(first, j) * size, size), size)
            attended = part_ref[at, columns(h)] + mm(q_ref[at, columns(h)], pair)
            mean = jnp.mean(attended * attended, axis=-1, keepdims=True)
            normed = attended * lax.rsqrt(mean + 1e-6) * gain_ref[:, columns(h)]
            out_refs[j][:, columns(h)] = normed.astype(BF16)


def normed_blocks(bit, other, q, part, base, got, gain, blocks):
    rows, width = q.shape
    return call(
        functools.partial(normed_kernel, bit, blocks, other),
        vm(q, part, base, got, gain),
        [((rows // blocks, width), BF16)] * (blocks // 2),
        flops=rows * width * DH,
    )


def weights_kernel(places, *refs):
    *parts, rest_ref, out_ref = refs
    for n, place in enumerate(places):
        for ref, other in ((parts[n], False), (parts[len(places) + n], True)):
            out_ref[pl.ds(share_row(*place, other), ref.shape[0]), :] = ref[...]
    left = rest_ref.shape[0]
    out_ref[pl.ds(out_ref.shape[0] - left, left), :] = rest_ref[...]


def join_weights(direct, neighbour, rest, places):
    rows = sum(part.shape[0] for part in (*direct, *neighbour, rest))
    return call(
        functools.partial(weights_kernel, places),
        vm(*direct, *neighbour, rest),
        [((rows, rest.shape[1]), BF16)],
        mib=8,
    )[0]


def project_own_kernel(w_ref, *refs):
    count = len(refs) // 2
    span = w_ref.shape[1]
    tile = 512 if span % 512 == 0 else span
    kept = jnp.concatenate([ref[...] for ref in refs[:count]], axis=0)
    size = kept.shape[0] // count
    for start in range(0, span, tile):
        at = slice(start, start + tile)
        total = mm(kept, w_ref[:, at])
        for n, out_ref in enumerate(refs[count:]):
            out_ref[:, at] = total[n * size : (n + 1) * size]


def project_own(kept, weight):
    size, width = kept[0].shape
    span = weight.shape[1]
    return call(
        project_own_kernel,
        vm(weight, *kept),
        [((size, span), F32)] * len(kept),
        flops=2 * len(kept) * size * width * span,
        mib=8,
    )


def project_kernel(own_ref, came_ref, w_ref, out_ref):
    span = out_ref.shape[1]
    tile = 512 if span % 512 == 0 else span
    for start in range(0, span, tile):
        at = slice(start, start + tile)
        out_ref[:, at] = (own_ref[:, at] + mm(came_ref[...], w_ref[:, at])).astype(out_ref.dtype)


def project(own, came, weight, dtype):
    size, span = own.shape
    return call(
        project_kernel,
        vm(own, came, weight),
        [((size, span), dtype)],
        flops=2 * size * came.shape[1] * span,
        mib=8,
    )[0]


def flip(value, axis, bit):
    count = lax.axis_size(axis)
    return lax.ppermute(value, axis, [(i, i ^ bit) for i in range(count)])


def shards(queries, key_vectors, value_vectors, norm_gain, out_weight):
    rows, width = queries.shape
    seq_count, head_count = lax.axis_size("seq"), lax.axis_size("head")
    block = 256 if rows % 256 == 0 else rows

    top = head_count // 2
    features = out_weight.shape[0]
    bits = [bit for n, bit in SHARES if bit < seq_count]
    sizes = [features * n // 32 // 16 * 16 for n, bit in SHARES if bit < seq_count]
    places = share_places(sizes, bits)

    q, k, v, sums, sums_send, *weight_shares = local_sums(
        queries, key_vectors, value_vectors, out_weight, sizes, places
    )
    pairs, pairs_send, paired, weight_rest = local_pairs(
        q, k, v, out_weight, features - 2 * sum(sizes), block
    )
    direct = [flip(w, "head", top) for w in weight_shares]
    neighbour = [flip(w, "seq", bits[n]) for n, w in enumerate(direct)]
    rest = flip(weight_rest, "head", top)
    heads = width // DH
    parts = [
        inner(q, k, v, paired, block, tuple(range(at, min(at + (heads + 1) // 2, heads))))
        for at in range(0, heads, (heads + 1) // 2)
    ]
    ahead = before = None
    bit = 1
    while 2 * bit < seq_count:
        sums_got = flip(sums_send, "seq", bit)
        pairs_got = flip(pairs_send, "seq", bit)
        last = 4 * bit >= seq_count
        old = ahead
        ahead, sums_send, *more_sums = union_sums(bit, sums_got, sums, ahead, heads, last)
        before, pairs_send, *more_pairs = union_pairs(
            bit, pairs_got, pairs, sums_got, sums, before, old, last
        )
        if not last:
            (pairs,), (sums,) = more_pairs, more_sums
        bit *= 2
    gram_got = flip(sums_send, "seq", bit)
    pairs_got = flip(pairs_send, "seq", bit)
    gram, base = ahead_of_device(bit, gram_got, ahead, before)
    part = outer(q, v, gram, parts, block)

    gain = norm_gain.reshape(1, width)
    sent = normed_blocks(bit, top, q, part, base, pairs_got, gain, head_count)
    came = [flip(rows_sent, "head", top) for rows_sent in sent]
    kept = normed_blocks(bit, 0, q, part, base, pairs_got, gain, head_count)
    own = project_own(kept, out_weight)
    weight_came = join_weights(direct, neighbour, rest, places)

    count = top
    results = {
        j: project(own[j], came[j], weight_came, BF16 if 2 * j >= count else F32)
        for j in reversed(range(count))
    }
    while count > 1:
        count //= 2
        for j in range(count):
            got = flip(results[count + j].astype(BF16), "head", count)
            results[j] = results[j].astype(F32) + got.astype(F32)
    return results[0].astype(BF16)


def solution(mesh):
    in_specs = (P("seq", "head"), P("seq", "head"), P("seq", "head"), P("head"), P("head", None))
    out_specs = P(("seq", "head"), None)

    return jax.shard_map(shards, mesh=mesh, in_specs=in_specs, out_specs=out_specs, check_vma=False)
```
